256 devices in a mesh: gx: 16 (over y_lo, z), gy: 16 (over y_hi, x, core).
Axes of the slice: x: 4, y: 4 (y_hi: 2, y_lo: 2; y = y_hi * 2 + y_lo), z: 8, core: 2. Of those that a mesh axis runs over, the one named last changes fastest.
Arguments:
- obs_values: bfloat16 [4096, 48, 128], P(('gx', 'gy')), may hold values from -1.5 to 1.5
- obs_weight: float32 [4096, 128], P(('gx', 'gy')), may hold values from 0.25 to 4
- obs_box: int32 [4096, 128], P(('gx', 'gy')), may hold values from 0 to 127
- obs_owner: int32 [4096], P(('gx', 'gy')), may hold values from 0 to 255
- block_count: int32 [256], P(('gx', 'gy')), may hold values from 1 to 16, as said below
- diff_x: float32 [48, 128, 2048], P(None, 'gx', 'gy'), may hold values from 0.02 to 0.24
- diff_y: float32 [48, 128, 2048], P(None, 'gx', 'gy'), may hold values from 0.02 to 0.24
- spread_std: float32 [48, 128, 2048], P(None, 'gx', 'gy'), may hold values from 0.3 to 3
- land_sea: int32 [128, 2048], P('gx', 'gy'), may hold values 0 or 1
- vert_corr: float32 [48, 48], replicated, may hold values from -0.12268693 to 1.122687, as said below
Outputs:
- increment: float32 [48, 128, 2048], P(None, 'gx', 'gy')
The draws below stay inside these ranges and needn't reach their ends.
Inputs may be any that keep to these rules, and one draw needn't show every extreme that they name: `block_count`: some device holds exactly 16 filled blocks in every draw. vert_corr is the identity plus a matrix E whose entries have magnitude at most 0.85 / sqrt(48); it is the same for all columns.
All inputs are finite; a program needn't handle non-finite values. No bound on the sum of `land_sea` on one device may be relied on, other than what follows from the above.
Results may differ from the reference program's by a relative error of at most 0.0003.
Values sent between devices are 32-bit elements; how exact they have to be, the bound alone decides.
A program may use at most 64 MiB of HBM per device.

```python
import math
import jax
import jax.numpy as jnp
from jax import lax

LEV = 48
CX = 8
CY = 128
OBS_BLK = 16
OBS_W = 128
BOX_DEV = 128
PASSES = 4
NX = 128
NY = 2048
OWNERS = 256
OBS_BLOCKS = 4096
N_GX = 16
N_GY = 16


def draw_vert_corr(key, part):
    noise = jnp.clip(0.5 * jax.random.normal(key, (LEV, LEV), jnp.float32), -0.85, 0.85)
    return jnp.eye(LEV, dtype=jnp.float32) + noise / LEV ** 0.5


def draw_block_count(key, part):
    first_key, second_key, third_key = jax.random.split(jax.random.fold_in(key, 7), 3)
    first = jax.random.randint(first_key, (OWNERS,), 1, OBS_BLK + 1)
    second = jax.random.randint(second_key, (OWNERS,), 1, OBS_BLK + 1)
    counts = jnp.clip(OBS_BLK // 2 + first * second // (2 * OBS_BLK), 1, OBS_BLK)
    where = jax.random.randint(third_key, (), 0, OWNERS)
    return counts.at[where].set(OBS_BLK).astype(jnp.int32)


def touch_ends(drawn, key, least, high):
    index_at = [jax.random.randint(jax.random.fold_in(key, axis), (), 0, length) for axis, length in enumerate(drawn.shape)]
    widest = drawn.shape.index(max(drawn.shape))
    next_to = index_at[:widest] + [(index_at[widest] + 1) % drawn.shape[widest]] + index_at[widest + 1:]
    return drawn.at[tuple(index_at)].set(least).at[tuple(next_to)].set(high)


def levels(rng, shape, cuts, low, top_value):
    level, own = 1.0, jax.random.fold_in(rng, 6)
    for dim, parts in cuts:
        draws = jnp.exp(jax.random.uniform(jax.random.fold_in(own, dim), (parts,), jnp.float32, low / len(cuts), top_value / len(cuts)))
        level = level * jnp.repeat(draws, shape[dim] // parts).reshape([-1 if axis == dim else 1 for axis in range(len(shape))])
    return level


def bell_draw(stream_key, dims, deviation, bound, shards=(), kind=jnp.bfloat16):
    values = deviation * jax.random.normal(stream_key, dims, jnp.float32)
    if shards:
        values = values * levels(stream_key, dims, shards, -0.22, 0.18)
    return jnp.clip(values, -bound, bound).astype(kind)


def setup_inputs(seed: int = 0) -> dict:
    splits = jax.random.split(jax.random.key(seed), 11)
    return {
        "obs_values": bell_draw(splits[0], (OBS_BLOCKS, LEV, OBS_W), 0.25, 1.5, ((0, 256),)),
        "obs_weight": jnp.clip(jnp.exp(math.log(4.0) - 2.7725887 * jax.random.uniform(splits[1], (OBS_BLOCKS, OBS_W), jnp.float32) ** levels(splits[1], (OBS_BLOCKS, OBS_W), ((0, 256),), -0.2, 0.2)), 0.25, 4.0),
        "obs_box": touch_ends(jax.random.randint(splits[2], (OBS_BLOCKS, OBS_W), 0, BOX_DEV), jax.random.fold_in(splits[2], 1), 0, BOX_DEV - 1).astype(jnp.int32),
        "obs_owner": touch_ends(jax.random.randint(splits[3], (OBS_BLOCKS,), 0, OWNERS), jax.random.fold_in(splits[3], 1), 0, OWNERS - 1).astype(jnp.int32),
        "block_count": draw_block_count(jax.random.fold_in(splits[10], 71), 0),
        "diff_x": jnp.clip(jnp.exp(math.log(0.24) - 2.4849066 * jax.random.uniform(splits[5], (LEV, NX, NY), jnp.float32) ** levels(splits[5], (LEV, NX, NY), ((1, 16), (2, 16)), -0.2, 0.2)), 0.02, 0.24),
        "diff_y": jnp.clip(jnp.exp(math.log(0.24) - 2.4849066 * jax.random.uniform(splits[6], (LEV, NX, NY), jnp.float32) ** levels(splits[6], (LEV, NX, NY), ((1, 16), (2, 16)), -0.2, 0.2)), 0.02, 0.24),
        "spread_std": jnp.clip(jnp.exp(math.log(3.0) - 2.3025851 * jax.random.uniform(splits[7], (LEV, NX, NY), jnp.float32) ** levels(splits[7], (LEV, NX, NY), ((1, 16), (2, 16)), -0.2, 0.2)), 0.3, 3.0),
        "land_sea": touch_ends((jax.random.randint(splits[8], (NX, NY), 0, 5) < 4).astype(jnp.int32), jax.random.fold_in(splits[8], 1), 0, 1),
        "vert_corr": draw_vert_corr(jax.random.fold_in(splits[10], 71), 0),
    }


HIGH = lax.Precision.HIGHEST


def one_pass(field, east, north):
    centre = field[:, 1:-1, 1:-1]
    out = centre + east[:, 1:-1, 1:-1] * (field[:, 2:, 1:-1] - centre)
    out = out + east[:, :-2, 1:-1] * (field[:, :-2, 1:-1] - centre)
    out = out + north[:, 1:-1, 1:-1] * (field[:, 1:-1, 2:] - centre)
    out = out + north[:, 1:-1, :-2] * (field[:, 1:-1, :-2] - centre)
    return out


def pad_grid(array):
    wrapped = jnp.concatenate([array[:, -1:], array, array[:, :1]], axis=1)
    return jnp.pad(wrapped, ((0, 0), (0, 0), (1, 1)))


def reference(obs_values, obs_weight, obs_box, obs_owner, block_count, diff_x, diff_y, spread_std, land_sea, vert_corr):
    values = obs_values.reshape(OWNERS, OBS_BLK, LEV, OBS_W)
    weights = obs_weight.reshape(OWNERS, OBS_BLK, OBS_W)
    boxes = obs_box.reshape(OWNERS, OBS_BLK, OBS_W)
    owners = obs_owner.reshape(OWNERS, OBS_BLK)
    filled = (jnp.arange(OBS_BLK, dtype=jnp.int32)[None, :] < block_count[:, None]).astype(jnp.float32)

    def add_source(total, item):
        vals, wts, bxs, own, full = item
        weighted = vals.astype(jnp.float32) * (wts * full[:, None])[:, None, :]
        target = (own[:, None] * BOX_DEV + bxs).reshape(-1)
        data = jnp.transpose(weighted, (0, 2, 1)).reshape(-1, LEV)
        return total + jax.ops.segment_sum(data, target, num_segments=OWNERS * BOX_DEV), None

    start = jnp.zeros((OWNERS * BOX_DEV, LEV), jnp.float32)
    superob, _ = lax.scan(add_source, start, (values, weights, boxes, owners, filled))
    superob = superob.reshape(OWNERS, BOX_DEV, LEV)
    vbox = jnp.einsum("lm,dkm->dlk", vert_corr, superob, precision=HIGH)
    grid = vbox.reshape(N_GX, N_GY, LEV, 8, 16)
    grid = jnp.transpose(grid, (2, 0, 3, 1, 4)).reshape(LEV, N_GX * 8, N_GY * 16)
    grid = jnp.repeat(jnp.repeat(grid, CX // 8, axis=1), CY // 16, axis=2)
    mask = land_sea.astype(jnp.float32)
    forcing = grid * spread_std * mask[None]
    mask_next_x = jnp.roll(mask, -1, axis=0)
    mask_next_y = jnp.concatenate([mask[:, 1:], jnp.zeros((NX, 1), jnp.float32)], axis=1)
    east = diff_x * (mask * mask_next_x)[None]
    north = diff_y * (mask * mask_next_y)[None]
    east_pad = pad_grid(east)
    north_pad = pad_grid(north)
    field = forcing
    for step in range(PASSES):
        field = one_pass(pad_grid(field), east_pad, north_pad)
    mixed = jnp.einsum("lm,mxy->lxy", vert_corr, field, precision=HIGH)
    return mixed * spread_std * mask[None]
```

```python
import jax
import jax.numpy as jnp
from jax import lax
from jax.sharding import PartitionSpec as P

BOX_DEV = 128
PASSES = 4


HIGH = lax.Precision.HIGHEST


def extended(block, sides, width):
    for axis, dim in sides:
        count = lax.axis_size(axis)
        forward = [(i, i + 1) for i in range(count - 1)]
        forward.append((count - 1, 0))
        backward = [(target, source) for source, target in forward]
        low = lax.ppermute(
            lax.slice_in_dim(block, block.shape[dim] - width, None, axis=dim), axis, forward
        )
        high = lax.ppermute(lax.slice_in_dim(block, 0, width, axis=dim), axis, backward)
        block = jnp.concatenate([low, block, high], axis=dim)
    return block


def one_pass(field, east, north):
    centre = field[:, 1:-1, 1:-1]
    out = centre + east[:, 1:-1, 1:-1] * (field[:, 2:, 1:-1] - centre)
    out = out + east[:, :-2, 1:-1] * (field[:, :-2, 1:-1] - centre)
    out = out + north[:, 1:-1, 1:-1] * (field[:, 1:-1, 2:] - centre)
    out = out + north[:, 1:-1, :-2] * (field[:, 1:-1, :-2] - centre)
    return out


def face_terms(padded, levels):
    diff_east = padded[:levels]
    diff_north = padded[levels : 2 * levels]
    mask = padded[2 * levels]
    east = diff_east[:, :-1, :] * (mask[:-1, :] * mask[1:, :])[None]
    north = diff_north[:, :, :-1] * (mask[:, :-1] * mask[:, 1:])[None]
    east = jnp.pad(east, ((0, 0), (0, 1), (0, 0)))
    north = jnp.pad(north, ((0, 0), (0, 0), (0, 1)))
    return (east, north)


def passes_round(padded, east, north):
    padded = one_pass(padded, east, north)
    return padded


def local(
    obs_values,
    obs_weight,
    obs_box,
    obs_owner,
    block_count,
    diff_x,
    diff_y,
    spread_std,
    land_sea,
    vert_corr,
):
    levels = diff_x.shape[0]
    width_x = diff_x.shape[1]
    width_y = diff_x.shape[2]
    blocks = obs_values.shape[0]
    box_count = BOX_DEV
    filled = (jnp.arange(blocks, dtype=jnp.int32) < block_count[0]).astype(jnp.float32)
    weighted = obs_values.astype(jnp.float32) * (obs_weight * filled[:, None])[:, None, :]
    onehot = (obs_box[:, :, None] == jnp.arange(box_count, dtype=jnp.int32)[None, None, :]).astype(
        jnp.float32
    )
    contrib = jnp.einsum("blo,bok->blk", weighted, onehot, precision=HIGH)
    by_level = lax.all_to_all(contrib, "gy", split_axis=1, concat_axis=0, tiled=True)
    owners = lax.all_gather(obs_owner, "gy", axis=0, tiled=True)
    targets = jnp.arange(lax.axis_size(("gx", "gy")) * 1, dtype=jnp.int32)
    select = (owners[None, :] == targets[:, None]).astype(jnp.float32)
    partial = jnp.einsum("rb,blk->rlk", select, by_level, precision=HIGH)
    mine = lax.psum_scatter(partial, "gx", scatter_dimension=0, tiled=True)
    superob = lax.all_to_all(mine, "gy", split_axis=0, concat_axis=1, tiled=True)[0]
    vbox = jnp.dot(vert_corr, superob, precision=HIGH)
    spread = vbox.reshape(levels, 8, 16)
    spread = jnp.repeat(jnp.repeat(spread, width_x // 8, axis=1), width_y // 16, axis=2)
    mask = land_sea.astype(jnp.float32)
    forcing = spread * spread_std * mask[None]
    depth = 1
    rounds = PASSES // depth
    moved = lax.all_to_all(
        jnp.stack([diff_x, diff_y]), "gy", split_axis=1, concat_axis=3, tiled=True
    )
    mask_whole = lax.all_gather(mask, "gy", axis=1, tiled=True)
    field = lax.all_to_all(forcing, "gy", split_axis=0, concat_axis=2, tiled=True)
    group = field.shape[0]
    stacked = jnp.concatenate([moved[0], moved[1], mask_whole[None]], axis=0)
    stacked = extended(stacked, (("gx", 1),), depth)
    stacked = jnp.pad(stacked, ((0, 0), (0, 0), (depth, depth)))
    east, north = face_terms(stacked, group)
    for turn in range(rounds):
        padded = extended(field, (("gx", 1),), depth)
        padded = jnp.pad(padded, ((0, 0), (0, 0), (depth, depth)))
        field = passes_round(padded, east, north)
    field = lax.all_to_all(field, "gy", split_axis=2, concat_axis=0, tiled=True)
    mixed = jnp.dot(vert_corr, field.reshape(levels, -1), precision=HIGH).reshape(
        levels, width_x, width_y
    )
    return mixed * spread_std * mask[None]


def solution(mesh):
    in_specs = (
        P(("gx", "gy"), None, None),
        P(("gx", "gy"), None),
        P(("gx", "gy"), None),
        P(("gx", "gy")),
        P(("gx", "gy")),
        P(None, "gx", "gy"),
        P(None, "gx", "gy"),
        P(None, "gx", "gy"),
        P("gx", "gy"),
        P(),
    )
    out_specs = P(None, "gx", "gy")
    return jax.shard_map(local, mesh=mesh, in_specs=in_specs, out_specs=out_specs, check_vma=False)
```

```python
import functools

import jax
import jax.numpy as jnp
from jax import lax
from jax.experimental import pallas as pl
from jax.experimental.pallas import tpu as pltpu
from jax.sharding import PartitionSpec as P

MESH = pl.DeviceIdType.MESH
F32 = jnp.float32
BF16 = jnp.bfloat16
LEV = 48
LANES = 128
PASSES = 4


def two_terms(x):
    high = x.astype(BF16)
    return high, (x - high.astype(F32)).astype(BF16)


def mul(a, b):
    return jnp.dot(a, b, preferred_element_type=F32)


def mul_terms(a, b):
    a_high, a_low = two_terms(a)
    b_high, b_low = two_terms(b)
    return mul(a_high, b_high) + mul(a_high, b_low) + mul(a_low, b_high)


def lane_of(shape):
    return lax.broadcasted_iota(jnp.int32, shape, len(shape) - 1)


def kernel(
    nz,
    ng,
    vals_hbm,
    weight,
    box,
    owner,
    count,
    dx_hbm,
    dy_hbm,
    sp_hbm,
    land,
    corr,
    out_hbm,
    vals,
    raw,
    ext,
    edge,
    pack_s,
    pack_r,
    slab_s,
    slab_r,
    sums_s,
    sums_r,
    own_s,
    own_r,
    part_s,
    part_r,
    tile_s,
    tile_r,
    box_s,
    box_r,
    field,
    out_v,
    local_sem,
    bulk_send,
    bulk_recv,
    pack_send,
    pack_recv,
    slab_send,
    slab_recv,
    all_send,
    all_recv,
    box_send,
    box_recv,
):
    group = 2 * ng
    per = LEV // ng
    rows1 = per * 8
    rows3 = tile_s.shape[0] // ng
    owners = nz * ng
    depth = group * 8
    gx = lax.axis_index("gx")
    gy = lax.axis_index("gy")
    half = lax.div(gx, nz)
    z = lax.rem(gx, nz)
    me = half * ng + gy

    def member(step):
        index = lax.rem(me + step, group)
        h = lax.div(index, ng)
        g = lax.rem(index, ng)
        return index, h, g, (h * nz + z, g)

    def along_z(step):
        target = lax.rem(z + step, nz)
        return target, (half * nz + target, gy)

    east = (lax.rem(gx + 1, 2 * nz), gy)
    west = (lax.rem(gx + 2 * nz - 1, 2 * nz), gy)
    north = (gx, lax.rem(gy + 1, ng))
    south = (gx, lax.rem(gy + ng - 1, ng))

    def remote(src, dst, send, recv, device):
        return pltpu.make_async_remote_copy(
            src_ref=src,
            dst_ref=dst,
            send_sem=send,
            recv_sem=recv,
            device_id=device,
            device_id_type=MESH,
        )

    loads = [
        pltpu.make_async_copy(dx_hbm, raw.at[0], local_sem.at[0]),
        pltpu.make_async_copy(dy_hbm, raw.at[1], local_sem.at[1]),
        pltpu.make_async_copy(sp_hbm, raw.at[2], local_sem.at[2]),
        pltpu.make_async_copy(vals_hbm, vals, local_sem.at[3]),
    ]
    for load in loads:
        load.start()

    barrier = pltpu.get_barrier_semaphore()

    def greet_plane(step, _):
        pl.semaphore_signal(barrier, inc=1, device_id=member(step)[3], device_id_type=MESH)
        return _

    def greet_z(step, _):
        pl.semaphore_signal(barrier, inc=1, device_id=along_z(step)[1], device_id_type=MESH)
        return _

    lax.fori_loop(1, group, greet_plane, 0)
    lax.fori_loop(1, nz, greet_z, 0)
    for device in (east, west):
        pl.semaphore_signal(barrier, inc=1, device_id=device, device_id_type=MESH)

    for load in loads[:3]:
        load.wait()
    mask = land[...].astype(F32)
    for x in range(8):
        for a in range(3):
            value = raw[a, pl.ds(x, LEV, stride=8), :]
            if a == 2:
                value = value * mask[x : x + 1, :]
            ext[4 + x, a] = value

    lane1 = lane_of((1, LANES))
    base = lax.rem(me * 8, LANES)
    for parity in range(2):
        row = jnp.zeros((1, LANES), jnp.int32)
        for j in range(8):
            row = jnp.where(lane1 == base + j, owner[2 * j + parity], row)
        own_s[parity : parity + 1, :] = row

    pl.semaphore_wait(barrier, group + nz)

    bulk = [
        remote(ext.at[pl.ds(4, 4)], ext.at[pl.ds(12, 4)], bulk_send.at[0], bulk_recv.at[0], west),
        remote(ext.at[pl.ds(8, 4)], ext.at[pl.ds(0, 4)], bulk_send.at[1], bulk_recv.at[1], east),
    ]
    for copy in bulk:
        copy.start()

    def send_owners(step, _):
        _, _, _, device = member(step)
        remote(own_s, own_r.at[me], all_send.at[0], all_recv.at[0], device).start()
        return _

    lax.fori_loop(1, group, send_owners, 0)
    own_r[me] = own_s[...]

    loads[3].wait()
    weighted = jnp.where(
        lax.broadcasted_iota(jnp.int32, (16, LANES), 0) < count[0], weight[...], 0.0
    )
    boxes = box[...]
    place = (boxes >> 6) * LANES + (boxes & 63)
    target = lax.broadcasted_iota(jnp.int32, (2 * LANES, LANES), 0)
    for j in range(8):
        terms = []
        hots = []
        for parity in range(2):
            b = 2 * j + parity
            value = vals[b].astype(F32) * weighted[b : b + 1, :]
            terms.append(two_terms(value))
            hit = target == place[b : b + 1, :] + 64 * parity
            hots.append(jnp.where(hit, 1.0, 0.0).astype(BF16))
        left = jnp.concatenate(
            [
                jnp.concatenate([terms[0][0], terms[1][0]], axis=1),
                jnp.concatenate([terms[0][1], terms[1][1]], axis=1),
            ],
            axis=0,
        )
        hot = jnp.concatenate(hots, axis=1)
        total = lax.dot_general(left, hot, (((1,), (1,)), ((), ())), preferred_element_type=F32)
        total = total[:LEV] + total[LEV:]
        sums_s[0, pl.ds(j, LEV, stride=8), :] = total[:, :LANES]
        sums_s[1, pl.ds(j, LEV, stride=8), :] = total[:, LANES:]

    def rows_of(g):
        return pl.ds(pl.multiple_of(g * rows1, 8), rows1)

    def send_sums(step, _):
        _, h, g, device = member(step)
        remote(
            sums_s.at[h, rows_of(g)], sums_r.at[me], all_send.at[1], all_recv.at[1], device
        ).start()
        return _

    lax.fori_loop(1, group, send_sums, 0)
    sums_r[me] = sums_s[half, rows_of(gy), :]

    lane = lane_of((LEV, LANES))
    for part in range(2):
        to_south = jnp.zeros((LEV, LANES), F32)
        to_north = jnp.zeros((LEV, LANES), F32)
        for r in range(4):
            for a in range(3):
                q = 3 * r + a
                value = ext[4 + 4 * part + r, a]
                if q:
                    value = pltpu.roll(value, 8 * q, 1)
                low = (8 * q + LANES - 4) % LANES
                to_south = jnp.where((lane >= 8 * q) & (lane < 8 * q + 4), value, to_south)
                to_north = jnp.where((lane >= low) & (lane < low + 4), value, to_north)
        pack_s[0, part] = to_south
        pack_s[1, part] = to_north
    packs = [
        remote(pack_s.at[0], pack_r.at[0], pack_send.at[0], pack_recv.at[0], south),
        remote(pack_s.at[1], pack_r.at[1], pack_send.at[1], pack_recv.at[1], north),
    ]
    for copy in packs:
        copy.start()

    level = lax.broadcasted_iota(jnp.int32, (LEV, ng * rows3), 0)
    column = lane_of((LEV, ng * rows3))
    from_group = column // rows3
    within = column - from_group * rows3
    own_level = (within < per) & (from_group * per + within == level)
    near_level = (
        (within >= per) & (within < 2 * per) & (from_group * per + within - per == level)
    )
    corr_v = corr[...]
    corr_rows = jnp.concatenate(
        [
            jnp.dot(
                corr_v,
                jnp.where(chosen, 1.0, 0.0),
                precision=lax.Precision.HIGHEST,
                preferred_element_type=F32,
            )
            for chosen in (own_level, near_level)
        ],
        axis=0,
    )

    for copy in packs:
        copy.wait()
    for part in range(2):
        from_north = jnp.where(gy < ng - 1, pack_r[0, part], 0.0)
        from_south = jnp.where(gy > 0, pack_r[1, part], 0.0)
        slab_s[part] = jnp.where((lane & 7) < 4, from_north, from_south)
    slabs = [
        remote(slab_s.at[0], slab_r.at[1], slab_send.at[0], slab_recv.at[0], west),
        remote(slab_s.at[1], slab_r.at[0], slab_send.at[1], slab_recv.at[1], east),
    ]
    for copy in slabs:
        copy.start()

    def wait_bytes(ref, sem, size):
        view = ref.at[pl.ds(0, size)]
        pltpu.make_async_copy(view, view, sem).wait()

    wait_bytes(own_r, all_recv.at[0], group - 1)
    wide = (depth + LANES - 1) // LANES
    owner_rows = []
    for parity in range(2):
        pieces = []
        for piece in range(wide):
            row = jnp.zeros((1, LANES), jnp.int32)
            for source in range(piece * 16, min(group, piece * 16 + 16)):
                row = row + own_r[source, parity : parity + 1, :]
            pieces.append(row)
        row = jnp.concatenate(pieces, axis=1) if wide > 1 else pieces[0]
        owner_rows.append(row[:, :depth])
    candidate = lax.broadcasted_iota(jnp.int32, (owners, depth), 0)
    hits = jnp.concatenate(
        [
            jnp.where(owner_rows[parity] == candidate + shift, 1.0, 0.0).astype(BF16)
            for parity, shift in ((0, 0), (1, 0), (1, owners), (0, owners))
        ],
        axis=1,
    )
    wait_bytes(sums_r, all_recv.at[1], group - 1)
    lower = lane_of((depth, LANES)) < 64
    columns = []
    for t in range(per):
        value = sums_r[:, t * 8 : t * 8 + 8, :].reshape(depth, LANES)
        other = pltpu.roll(value, 64, 1)
        columns.append(
            jnp.concatenate(
                [
                    jnp.where(lower, value, 0.0),
                    jnp.where(lower, other, 0.0),
                    jnp.where(lower, 0.0, value),
                    jnp.where(lower, 0.0, other),
                ],
                axis=0,
            )
        )
    stack_high, stack_low = two_terms(jnp.concatenate(columns, axis=1))
    by_owner = mul(hits, stack_high) + mul(hits, stack_low)
    for t in range(per):
        part_s[:, t] = by_owner[:, t * LANES : (t + 1) * LANES].reshape(nz, ng, LANES)

    def send_parts(step, _):
        index, device = along_z(step)
        remote(
            part_s.at[index], part_r.at[z], all_send.at[2], all_recv.at[2], device
        ).start()
        return _

    lax.fori_loop(1, nz, send_parts, 0)
    part_r[z] = part_s[z]

    for copy in slabs:
        copy.wait()
    outer = (lane < 4) | (lane >= LANES - 4)
    for part in range(4):
        slab = (slab_r[0], slab_s[0], slab_s[1], slab_r[1])[part]
        for r in range(4):
            for a in range(3):
                q = 3 * r + a
                value = pltpu.roll(slab, LANES - 8 * q, 1) if q else slab
                edge[4 * part + r, a] = jnp.where(outer, value, 0.0)
    for copy in bulk:
        copy.wait()

    def faces(x, _):
        here, beyond = ext[x, 2], edge[x, 2]
        last = lane == LANES - 1
        turned, turned_beyond = pltpu.roll(here, LANES - 1, 1), pltpu.roll(beyond, LANES - 1, 1)
        ext[x, 0] = jnp.where(here * ext[x + 1, 2] > 0.0, ext[x, 0], 0.0)
        edge[x, 0] = jnp.where(beyond * edge[x + 1, 2] > 0.0, edge[x, 0], 0.0)
        upper = jnp.where(last, turned_beyond, turned)
        upper_beyond = jnp.where(last, turned, turned_beyond)
        ext[x, 1] = jnp.where(here * upper > 0.0, ext[x, 1], 0.0)
        edge[x, 1] = jnp.where(beyond * upper_beyond > 0.0, edge[x, 1], 0.0)
        return _

    lax.fori_loop(0, 15, faces, 0)

    wait_bytes(part_r, all_recv.at[2], nz - 1)
    tile_s[...] = jnp.zeros(tile_s.shape, F32)
    row = lax.broadcasted_iota(jnp.int32, (ng, LANES), 0)
    box_column = lane_of((ng, LANES)) & 15
    for t in range(per):
        value = part_r[0, t]
        for source in range(1, nz):
            value = value + part_r[source, t]
        below = jnp.where(row == 0, 0.0, pltpu.roll(value, 1, 0))
        above = jnp.where(row == ng - 1, 0.0, pltpu.roll(value, ng - 1, 0))
        tile_s[pl.ds(t, ng, stride=rows3), :] = value
        tile_s[pl.ds(per + t, ng, stride=rows3), :] = jnp.where(box_column == 15, below, above)

    def tile_rows(g):
        return pl.ds(pl.multiple_of(g * rows3, 8), rows3)

    def send_tiles(step, _):
        _, _, g, device = member(step)
        remote(
            tile_s.at[tile_rows(g)], tile_r.at[me], all_send.at[3], all_recv.at[3], device
        ).start()
        return _

    lax.fori_loop(1, group, send_tiles, 0)
    tile_r[me] = tile_s[tile_rows(gy), :]

    wait_bytes(tile_r, all_recv.at[3], group - 1)
    arrived = jnp.concatenate(
        [tile_r[h * ng : (h + 1) * ng].reshape(ng * rows3, LANES) for h in range(2)], axis=1
    )
    mixed = mul_terms(corr_rows, arrived)
    for h in range(2):
        mine = mixed[:LEV, h * LANES : (h + 1) * LANES]
        near = mixed[LEV:, h * LANES : (h + 1) * LANES]
        turned = pltpu.roll(jnp.where(half == 0, near, mine), 64, 1)
        low_part = jnp.where(half == 0, mine, turned)
        high_part = jnp.where(half == 0, turned, near)
        box_s[h] = jnp.where(lane < 64, low_part, high_part)
    borders = [
        remote(box_s.at[0], box_r.at[1], box_send.at[0], box_recv.at[0], west),
        remote(box_s.at[1], box_r.at[0], box_send.at[1], box_recv.at[1], east),
    ]
    for copy in borders:
        copy.start()
    for copy in borders:
        copy.wait()

    lane8 = lane_of((8, LANES))
    first, last = lane8 == 0, lane8 == LANES - 1

    def advance(step, _):
        rows = pl.ds(pl.multiple_of(step * 8, 8), 8)
        inner, outside = [], []
        for part in range(4):
            source = (box_r.at[0], box_s.at[0], box_s.at[1], box_r.at[1])[part]
            value = source[rows, :]
            for r in range(4):
                x = 4 * part + r
                at_inner = 16 * r + (lane8 >> 3)
                at_outside = jnp.where(lane8 < 64, 64 + 16 * r, 64 + 16 * r + 15)
                inner.append(ext[x, 2, rows, :] * jnp.take_along_axis(value, at_inner, axis=1))
                outside.append(
                    edge[x, 2, rows, :] * jnp.take_along_axis(value, at_outside, axis=1)
                )
        for turn in range(PASSES):
            low, high = 1 + turn, 15 - turn
            flow = {}
            for x in range(low - 1, high):
                flow[x] = (
                    ext[x, 0, rows, :] * (inner[x + 1] - inner[x]),
                    edge[x, 0, rows, :] * (outside[x + 1] - outside[x]),
                )
            new_inner, new_outside = list(inner), list(outside)
            for x in range(low, high):
                here, beyond = inner[x], outside[x]
                turned = pltpu.roll(here, LANES - 1, 1)
                turned_beyond = pltpu.roll(beyond, LANES - 1, 1)
                up = ext[x, 1, rows, :] * (jnp.where(last, turned_beyond, turned) - here)
                up_beyond = edge[x, 1, rows, :] * (
                    jnp.where(last, turned, turned_beyond) - beyond
                )
                back, back_beyond = pltpu.roll(up, 1, 1), pltpu.roll(up_beyond, 1, 1)
                down = jnp.where(first, back_beyond, back)
                down_beyond = jnp.where(first, back, back_beyond)
                new_inner[x] = here + (flow[x][0] - flow[x - 1][0]) + (up - down)
                new_outside[x] = beyond + (flow[x][1] - flow[x - 1][1]) + (up_beyond - down_beyond)
            inner, outside = new_inner, new_outside
        for x in range(8):
            field[x, rows, :] = inner[4 + x]
        return _

    lax.fori_loop(0, LEV // 8, advance, 0)

    whole = jnp.concatenate([field[x] for x in range(8)], axis=1)
    result = mul_terms(corr_v, whole)
    for x in range(8):
        out_v[pl.ds(x, LEV, stride=8), :] = ext[4 + x, 2] * result[:, x * LANES : (x + 1) * LANES]
    store = pltpu.make_async_copy(out_v, out_hbm, local_sem.at[4])
    store.start()

    def wait_sent(ref, sem, size):
        view = ref.at[pl.ds(0, size)]
        pltpu.make_async_copy(view, view, sem).wait()

    wait_sent(own_r, all_send.at[0], group - 1)
    wait_sent(sums_r, all_send.at[1], group - 1)
    wait_sent(part_r, all_send.at[2], nz - 1)
    wait_sent(tile_r, all_send.at[3], group - 1)
    store.wait()


def local(
    nz,
    ng,
    obs_values,
    obs_weight,
    obs_box,
    obs_owner,
    block_count,
    diff_x,
    diff_y,
    spread_std,
    land_sea,
    vert_corr,
):
    group = 2 * ng
    per = LEV // ng
    rows3 = -(-2 * per // 8) * 8
    vmem = pl.BlockSpec(memory_space=pltpu.VMEM)
    smem = pl.BlockSpec(memory_space=pltpu.SMEM)
    hbm = pl.BlockSpec(memory_space=pl.ANY)
    dma = pltpu.SemaphoreType.DMA
    flat = (LEV * 8, LANES)
    out = pl.pallas_call(
        functools.partial(kernel, nz, ng),
        out_shape=jax.ShapeDtypeStruct(flat, F32),
        in_specs=[hbm, vmem, vmem, smem, smem, hbm, hbm, hbm, vmem, vmem],
        out_specs=hbm,
        scratch_shapes=[
            pltpu.VMEM((16, LEV, LANES), BF16),
            pltpu.VMEM((3,) + flat, F32),
            pltpu.VMEM((16, 3, LEV, LANES), F32),
            pltpu.VMEM((16, 3, LEV, LANES), F32),
            pltpu.VMEM((2, 2, LEV, LANES), F32),
            pltpu.VMEM((2, 2, LEV, LANES), F32),
            pltpu.VMEM((2, LEV, LANES), F32),
            pltpu.VMEM((2, LEV, LANES), F32),
            pltpu.VMEM((2,) + flat, F32),
            pltpu.VMEM((group, per * 8, LANES), F32),
            pltpu.VMEM((2, LANES), jnp.int32),
            pltpu.VMEM((group, 2, LANES), jnp.int32),
            pltpu.VMEM((nz, per, ng, LANES), F32),
            pltpu.VMEM((nz, per, ng, LANES), F32),
            pltpu.VMEM((ng * rows3, LANES), F32),
            pltpu.VMEM((group, rows3, LANES), F32),
            pltpu.VMEM((2, LEV, LANES), F32),
            pltpu.VMEM((2, LEV, LANES), F32),
            pltpu.VMEM((8, LEV, LANES), F32),
            pltpu.VMEM(flat, F32),
            dma((5,)),
            dma((2,)),
            dma((2,)),
            dma((2,)),
            dma((2,)),
            dma((2,)),
            dma((2,)),
            dma((4,)),
            dma((4,)),
            dma((2,)),
            dma((2,)),
        ],
        compiler_params=pltpu.CompilerParams(
            collective_id=0, has_side_effects=True, vmem_limit_bytes=40 * 1024 * 1024
        ),
        name="analysis",
    )(
        obs_values,
        obs_weight,
        obs_box,
        obs_owner,
        block_count,
        diff_x.reshape(flat),
        diff_y.reshape(flat),
        spread_std.reshape(flat),
        land_sea,
        vert_corr,
    )
    return out.reshape(LEV, 8, LANES)


def solution(mesh):
    in_specs = (
        P(("gx", "gy"), None, None),
        P(("gx", "gy"), None),
        P(("gx", "gy"), None),
        P(("gx", "gy")),
        P(("gx", "gy")),
        P(None, "gx", "gy"),
        P(None, "gx", "gy"),
        P(None, "gx", "gy"),
        P("gx", "gy"),
        P(),
    )
    return jax.shard_map(
        functools.partial(local, mesh.shape["gx"] // 2, mesh.shape["gy"]),
        mesh=mesh,
        in_specs=in_specs,
        out_specs=P(None, "gx", "gy"),
        check_vma=False,
    )
```

```python
import functools

import jax
import jax.numpy as jnp
from jax import lax
from jax.experimental import pallas as pl
from jax.experimental.pallas import tpu as pltpu
from jax.sharding import PartitionSpec as P

MESH = pl.DeviceIdType.MESH
F32 = jnp.float32
BF16 = jnp.bfloat16
LEV = 48
LANES = 128
PASSES = 4
NEAR = 2
CHUNK = 16


def two_terms(x):
    high = x.astype(BF16)
    return high, (x - high.astype(F32)).astype(BF16)


def mul(a, b):
    return jnp.dot(a, b, preferred_element_type=F32)


def mul_terms(a, b):
    a_high, a_low = two_terms(a)
    b_high, b_low = two_terms(b)
    return mul(a_high, b_high) + mul(a_high, b_low) + mul(a_low, b_high)


def lane_of(shape):
    return lax.broadcasted_iota(jnp.int32, shape, len(shape) - 1)


def kernel(
    nz,
    ng,
    count,
    vals_hbm,
    weight_hbm,
    box_hbm,
    owner_hbm,
    dx_hbm,
    dy_hbm,
    sp_hbm,
    land_hbm,
    corr_hbm,
    out_v,
    weight,
    box,
    owner,
    land,
    corr,
    vals,
    raw,
    ext,
    edge,
    pack_s,
    pack_r,
    slab_s,
    slab_r,
    sums_s,
    sums_r,
    by_level,
    part_s,
    part_r,
    tile_s,
    tile_r,
    box_s,
    box_r,
    field,
    face_below,
    local_sem,
    bulk_send,
    bulk_recv,
    pack_send,
    pack_recv,
    slab_send,
    slab_recv,
    all_send,
    all_recv,
    box_send,
    box_recv,
):
    group = 2 * ng
    per = LEV // ng
    rows1 = per * 8
    rows3 = tile_r.shape[1]
    sent3 = -(-per // 4) * 4
    owners = nz * ng
    depth = group * 8
    gx = lax.axis_index("gx")
    gy = lax.axis_index("gy")
    half = lax.div(gx, nz)
    z = lax.rem(gx, nz)
    me = half * ng + gy

    def member(step):
        index = lax.rem(me + step, group)
        h = lax.div(index, ng)
        g = lax.rem(index, ng)
        return index, h, g, (h * nz + z, g)

    def along_z(step):
        target = lax.rem(z + step, nz)
        return target, (half * nz + target, gy)

    east = (lax.rem(gx + 1, 2 * nz), gy)
    west = (lax.rem(gx + 2 * nz - 1, 2 * nz), gy)
    north = (gx, lax.rem(gy + 1, ng))
    south = (gx, lax.rem(gy + ng - 1, ng))

    def remote(src, dst, send, recv, device):
        return pltpu.make_async_remote_copy(
            src_ref=src,
            dst_ref=dst,
            send_sem=send,
            recv_sem=recv,
            device_id=device,
            device_id_type=MESH,
        )

    tile_r[...] = jnp.zeros(tile_r.shape, F32)
    tile_s[...] = jnp.zeros(tile_s.shape, F32)
    loads = [
        pltpu.make_async_copy(owner_hbm, owner, local_sem.at[0]),
        pltpu.make_async_copy(weight_hbm, weight, local_sem.at[1]),
        pltpu.make_async_copy(box_hbm, box, local_sem.at[2]),
        pltpu.make_async_copy(vals_hbm, vals, local_sem.at[3]),
        pltpu.make_async_copy(land_hbm, land, local_sem.at[4]),
        pltpu.make_async_copy(dx_hbm, raw.at[0], local_sem.at[5]),
        pltpu.make_async_copy(dy_hbm, raw.at[1], local_sem.at[6]),
        pltpu.make_async_copy(sp_hbm, raw.at[2], local_sem.at[7]),
        pltpu.make_async_copy(corr_hbm, corr, local_sem.at[8]),
    ]
    for load in loads[:4]:
        load.start()

    barrier = pltpu.get_barrier_semaphore()

    def greet_plane(step, _):
        pl.semaphore_signal(barrier, inc=1, device_id=member(step)[3], device_id_type=MESH)
        return _

    def greet_z(step, _):
        pl.semaphore_signal(barrier, inc=1, device_id=along_z(step)[1], device_id_type=MESH)
        return _

    lax.fori_loop(1, group, greet_plane, 0)
    lax.fori_loop(1, nz, greet_z, 0)
    for device in (east, west):
        pl.semaphore_signal(barrier, inc=1, device_id=device, device_id_type=MESH)
    for load in loads[4:]:
        load.start()

    for load in loads[:4]:
        load.wait()
    weighted = jnp.where(
        lax.broadcasted_iota(jnp.int32, (16, LANES), 0) < count[0], weight[...], 0.0
    )
    boxes = box[...]
    place = (boxes >> 6) * LANES + (boxes & 63)
    target = lax.broadcasted_iota(jnp.int32, (2 * LANES, LANES), 0)
    for j in range(8):
        terms = []
        hots = []
        for parity in range(2):
            b = 2 * j + parity
            value = vals[b].astype(F32) * weighted[b : b + 1, :]
            terms.append(two_terms(value))
            hit = target == place[b : b + 1, :] + 64 * parity
            hots.append(jnp.where(hit, 1.0, 0.0).astype(BF16))
        left = jnp.concatenate(
            [
                jnp.concatenate([terms[0][0], terms[1][0]], axis=1),
                jnp.concatenate([terms[0][1], terms[1][1]], axis=1),
            ],
            axis=0,
        )
        hot = jnp.concatenate(hots, axis=1)
        total = lax.dot_general(left, hot, (((1,), (1,)), ((), ())), preferred_element_type=F32)
        total = total[:LEV] + total[LEV:]
        by_level[0, pl.ds(j, LEV, stride=8), :] = total[:, :LANES]
        by_level[1, pl.ds(j, LEV, stride=8), :] = total[:, LANES:]

    lane1 = lane_of((1, LANES))
    base = lax.rem(me * 8, LANES)
    base_odd = lax.rem(me * 8 + 64, LANES)
    owner_row = jnp.zeros((1, LANES), F32)
    for j in range(8):
        owner_row = jnp.where(lane1 == base + j, owner[2 * j].astype(F32), owner_row)
        owner_row = jnp.where(lane1 == base_odd + j, owner[2 * j + 1].astype(F32), owner_row)
    for h in range(2):
        for g in range(ng):
            sums_s[h * ng + g, 0:rows1, :] = by_level[h, g * rows1 : (g + 1) * rows1, :]
            sums_s[h * ng + g, rows1 : rows1 + 1, :] = owner_row

    for load in loads[4:]:
        load.wait()
    mask = land[...].astype(F32)
    for x in range(8):
        for a in range(3):
            value = raw[a, pl.ds(x, LEV, stride=8), :]
            if a == 2:
                value = value * mask[x : x + 1, :]
            ext[4 + x, a] = value

    lane = lane_of((LEV, LANES))
    for part in range(2):
        to_south = jnp.zeros((LEV, LANES), F32)
        to_north = jnp.zeros((LEV, LANES), F32)
        for r in range(4):
            for a in range(3):
                q = 3 * r + a
                value = ext[4 + 4 * part + r, a]
                if q:
                    value = pltpu.roll(value, 8 * q, 1)
                low = (8 * q + LANES - 4) % LANES
                to_south = jnp.where((lane >= 8 * q) & (lane < 8 * q + 4), value, to_south)
                to_north = jnp.where((lane >= low) & (lane < low + 4), value, to_north)
        pack_s[0, part] = to_south
        pack_s[1, part] = to_north
    packs = [
        remote(pack_s.at[0], pack_r.at[0], pack_send.at[0], pack_recv.at[0], south),
        remote(pack_s.at[1], pack_r.at[1], pack_send.at[1], pack_recv.at[1], north),
    ]
    pl.semaphore_wait(barrier, group + nz)
    for copy in packs:
        copy.start()


    def send_sums(step, _):
        index, _, _, device = member(step)
        remote(
            sums_s.at[index], sums_r.at[me], all_send.at[0], all_recv.at[0], device
        ).start()
        return 0

    lax.fori_loop(1, group, send_sums, 0)
    sums_r[me] = sums_s[me]

    for copy in packs:
        copy.wait()
    for part in range(2):
        from_north = jnp.where(gy < ng - 1, pack_r[0, part], 0.0)
        from_south = jnp.where(gy > 0, pack_r[1, part], 0.0)
        slab_s[part] = jnp.where((lane & 7) < 4, from_north, from_south)
    slabs = [
        remote(slab_s.at[0], slab_r.at[1], slab_send.at[0], slab_recv.at[0], west),
        remote(slab_s.at[1], slab_r.at[0], slab_send.at[1], slab_recv.at[1], east),
    ]
    for copy in slabs:
        copy.start()
    def rows_to_neighbours(index, low, size):
        return [
            remote(
                ext.at[pl.ds(4 + low, size)],
                ext.at[pl.ds(12 + low, size)],
                bulk_send.at[index, 0],
                bulk_recv.at[index, 0],
                west,
            ),
            remote(
                ext.at[pl.ds(12 - low - size, size)],
                ext.at[pl.ds(4 - low - size, size)],
                bulk_send.at[index, 1],
                bulk_recv.at[index, 1],
                east,
            ),
        ]

    bulk = rows_to_neighbours(0, 0, NEAR)
    for copy in bulk:
        copy.start()

    level = lax.broadcasted_iota(jnp.int32, (LEV, ng * rows3), 0)
    column = lane_of((LEV, ng * rows3))
    from_group = column // rows3
    within = column - from_group * rows3
    chosen = (within < per) & (from_group * per + within == level)
    corr_v = corr[...]
    corr_rows = jnp.dot(
        corr_v,
        jnp.where(chosen, 1.0, 0.0),
        precision=lax.Precision.HIGHEST,
        preferred_element_type=F32,
    )

    for copy in slabs:
        copy.wait()
    outer = (lane < 4) | (lane >= LANES - 4)
    for part in range(4):
        slab = (slab_r[0], slab_s[0], slab_s[1], slab_r[1])[part]
        for r in range(4):
            for a in range(3):
                q = 3 * r + a
                value = pltpu.roll(slab, LANES - 8 * q, 1) if q else slab
                edge[4 * part + r, a] = jnp.where(outer, value, 0.0)

    def wait_bytes(ref, sem, size):
        view = ref.at[pl.ds(0, size)]
        pltpu.make_async_copy(view, view, sem).wait()

    wait_bytes(sums_r, all_recv.at[0], group - 1)
    wide = (depth + LANES - 1) // LANES
    owner_rows = []
    for parity in range(2):
        pieces = []
        for piece in range(wide):
            row = jnp.zeros((1, LANES), F32)
            for source in range(piece * 16, min(group, piece * 16 + 16)):
                start = (source * 8 + 64 * parity) % LANES
                row = jnp.where(
                    (lane1 >= start) & (lane1 < start + 8),
                    sums_r[source, rows1 : rows1 + 1, :],
                    row,
                )
            pieces.append(pltpu.roll(row, 64, 1) if parity else row)
        row = jnp.concatenate(pieces, axis=1) if wide > 1 else pieces[0]
        owner_rows.append(row[:, :depth])
    candidate = lax.broadcasted_iota(jnp.int32, (owners, depth), 0)
    even, odd = (row.astype(jnp.int32) for row in owner_rows)

    def hits(row, shift):
        return jnp.where(row == candidate + shift, 1.0, 0.0).astype(BF16)

    left = jnp.concatenate(
        [
            jnp.concatenate([hits(even, 0), hits(odd, 0)], axis=1),
            jnp.concatenate([hits(odd, owners), hits(even, owners)], axis=1),
        ],
        axis=0,
    )
    columns = []
    for t in range(per):
        value = sums_r[:, t * 8 : t * 8 + 8, :].reshape(depth, LANES)
        columns.append(jnp.concatenate([value, pltpu.roll(value, 64, 1)], axis=0))
    stack_high, stack_low = two_terms(jnp.concatenate(columns, axis=1))
    by_owner = mul(left, stack_high) + mul(left, stack_low)
    lower = lane_of((owners, LANES)) < 64
    for t in range(per):
        cut = by_owner[:, t * LANES : (t + 1) * LANES]
        part_s[:, t] = jnp.where(lower, cut[:owners], cut[owners:]).reshape(nz, ng, LANES)

    def send_parts(step, _):
        index, device = along_z(step)
        remote(
            part_s.at[index], part_r.at[z], all_send.at[1], all_recv.at[1], device
        ).start()
        return _

    lax.fori_loop(1, nz, send_parts, 0)
    part_r[z] = part_s[z]

    for copy in bulk:
        copy.wait()

    def faces(x, _):
        here, beyond = ext[x, 2], edge[x, 2]
        last = lane == LANES - 1
        turned, turned_beyond = pltpu.roll(here, LANES - 1, 1), pltpu.roll(beyond, LANES - 1, 1)
        ext[x, 0] = jnp.where(here * ext[x + 1, 2] > 0.0, ext[x, 0], 0.0)
        edge[x, 0] = jnp.where(beyond * edge[x + 1, 2] > 0.0, edge[x, 0], 0.0)
        upper = jnp.where(last, turned_beyond, turned)
        upper_beyond = jnp.where(last, turned, turned_beyond)
        north_face = jnp.where(here * upper > 0.0, ext[x, 1], 0.0)
        north_face_beyond = jnp.where(beyond * upper_beyond > 0.0, edge[x, 1], 0.0)
        turned, turned_beyond = pltpu.roll(north_face, 1, 1), pltpu.roll(north_face_beyond, 1, 1)
        ext[x, 1] = north_face
        edge[x, 1] = north_face_beyond
        face_below[x, 0] = jnp.where(lane == 0, turned_beyond, turned)
        face_below[x, 1] = jnp.where(lane == 0, turned, turned_beyond)
        return _

    lax.fori_loop(4 - NEAR, 11 + NEAR, faces, 0)

    wait_bytes(part_r, all_recv.at[1], nz - 1)
    row = lax.broadcasted_iota(jnp.int32, (ng, LANES), 0)
    box_column = lane_of((ng, LANES)) & 15
    low_boxes = lane_of((ng, LANES)) < 64
    for t in range(per):
        value = part_r[0, t]
        for source in range(1, nz):
            value = value + part_r[source, t]
        below = jnp.where(row == 0, 0.0, pltpu.roll(value, 1, 0))
        above = jnp.where(row == ng - 1, 0.0, pltpu.roll(value, ng - 1, 0))
        near = jnp.where(box_column == 15, below, above)
        other, other_near = pltpu.roll(value, 64, 1), pltpu.roll(near, 64, 1)
        tile_s[pl.ds(t, ng, stride=rows3), :] = jnp.where(low_boxes, value, other_near)
        tile_s[pl.ds(ng * rows3 + t, ng, stride=rows3), :] = jnp.where(low_boxes, other, near)

    def send_tiles(step, _):
        index, _, _, device = member(step)
        start = pl.multiple_of(index * rows3, 8)
        remote(
            tile_s.at[pl.ds(start, sent3)],
            tile_r.at[me, pl.ds(0, sent3)],
            all_send.at[2],
            all_recv.at[2],
            device,
        ).start()
        return 0

    lax.fori_loop(1, group, send_tiles, 0)
    far = rows_to_neighbours(1, NEAR, 4 - NEAR)
    for copy in far:
        copy.start()
    tile_r[me] = tile_s[pl.ds(pl.multiple_of(me * rows3, 8), rows3), :]

    wait_bytes(tile_r.at[:, pl.ds(0, sent3)], all_recv.at[2], group - 1)
    arrived = jnp.concatenate(
        [tile_r[h * ng : (h + 1) * ng].reshape(ng * rows3, LANES) for h in range(2)], axis=1
    )
    mixed = mul_terms(corr_rows, arrived)
    for h in range(2):
        box_s[h] = mixed[:, h * LANES : (h + 1) * LANES]
    borders = [
        remote(box_s.at[0], box_r.at[1], box_send.at[0], box_recv.at[0], west),
        remote(box_s.at[1], box_r.at[0], box_send.at[1], box_recv.at[1], east),
    ]
    for copy in borders:
        copy.start()
    for copy in far:
        copy.wait()
    lax.fori_loop(0, 4 - NEAR, faces, 0)
    lax.fori_loop(11 + NEAR, 15, faces, 0)
    for copy in borders:
        copy.wait()

    lane8 = lane_of((CHUNK, LANES))
    first, last = lane8 == 0, lane8 == LANES - 1

    def advance(step, _):
        rows = pl.ds(pl.multiple_of(step * CHUNK, 8), CHUNK)
        inner, outside = [], []
        for part in range(4):
            source = (box_r.at[0], box_s.at[0], box_s.at[1], box_r.at[1])[part]
            value = source[rows, :]
            for r in range(4):
                x = 4 * part + r
                at_inner = 16 * r + (lane8 >> 3)
                at_outside = jnp.where(lane8 < 64, 64 + 16 * r, 64 + 16 * r + 15)
                inner.append(ext[x, 2, rows, :] * jnp.take_along_axis(value, at_inner, axis=1))
                outside.append(
                    edge[x, 2, rows, :] * jnp.take_along_axis(value, at_outside, axis=1)
                )
        for turn in range(PASSES):
            low, high = 1 + turn, 15 - turn
            final = turn == PASSES - 1
            turned = {}
            for x in range(low, high):
                turned[x] = [
                    pltpu.roll(value[x], shift, 1)
                    for shift in (LANES - 1, 1)
                    for value in (inner, outside)
                ]
            flow = {}
            for x in range(low - 1, high):
                flow[x] = ext[x, 0, rows, :] * (inner[x + 1] - inner[x])
            new_inner, new_outside = list(inner), list(outside)
            for x in range(low, high):
                here = inner[x]
                above, above_beyond, below, below_beyond = turned[x]
                up = ext[x, 1, rows, :] * (jnp.where(last, above_beyond, above) - here)
                down = face_below[x, 0, rows, :] * (jnp.where(first, below_beyond, below) - here)
                new_inner[x] = here + (flow[x] - flow[x - 1]) + (up + down)
            if not final:
                for x in range(low - 1, high):
                    flow[x] = edge[x, 0, rows, :] * (outside[x + 1] - outside[x])
                for x in range(low, high):
                    here = outside[x]
                    above, above_beyond, below, below_beyond = turned[x]
                    up = edge[x, 1, rows, :] * (jnp.where(last, above, above_beyond) - here)
                    down = face_below[x, 1, rows, :] * (
                        jnp.where(first, below, below_beyond) - here
                    )
                    new_outside[x] = here + (flow[x] - flow[x - 1]) + (up + down)
            inner, outside = new_inner, new_outside
        for x in range(8):
            field[x, rows, :] = inner[4 + x]
        return _

    lax.fori_loop(0, LEV // CHUNK, advance, 0)

    whole = jnp.concatenate([field[x] for x in range(8)], axis=1)
    result = mul_terms(corr_v, whole)
    for x in range(8):
        out_v[pl.ds(x, LEV, stride=8), :] = ext[4 + x, 2] * result[:, x * LANES : (x + 1) * LANES]

    wait_bytes(sums_r, all_send.at[0], group - 1)
    wait_bytes(part_r, all_send.at[1], nz - 1)
    wait_bytes(tile_r.at[:, pl.ds(0, sent3)], all_send.at[2], group - 1)


def local(
    nz,
    ng,
    obs_values,
    obs_weight,
    obs_box,
    obs_owner,
    block_count,
    diff_x,
    diff_y,
    spread_std,
    land_sea,
    vert_corr,
):
    group = 2 * ng
    per = LEV // ng
    rows3 = -(-per // 8) * 8
    hbm = pl.BlockSpec(memory_space=pltpu.HBM)
    dma = pltpu.SemaphoreType.DMA
    flat = (LEV * 8, LANES)
    out = pl.pallas_call(
        functools.partial(kernel, nz, ng),
        out_shape=jax.ShapeDtypeStruct(flat, F32),
        in_specs=[pl.BlockSpec(memory_space=pltpu.SMEM)] + [hbm] * 9,
        out_specs=pl.BlockSpec(memory_space=pltpu.VMEM),
        scratch_shapes=[
            pltpu.VMEM((16, LANES), F32),
            pltpu.VMEM((16, LANES), jnp.int32),
            pltpu.SMEM((16,), jnp.int32),
            pltpu.VMEM((8, LANES), jnp.int32),
            pltpu.VMEM((LEV, LEV), F32),
            pltpu.VMEM((16, LEV, LANES), BF16),
            pltpu.VMEM((3,) + flat, F32),
            pltpu.VMEM((16, 3, LEV, LANES), F32),
            pltpu.VMEM((16, 3, LEV, LANES), F32),
            pltpu.VMEM((2, 2, LEV, LANES), F32),
            pltpu.VMEM((2, 2, LEV, LANES), F32),
            pltpu.VMEM((2, LEV, LANES), F32),
            pltpu.VMEM((2, LEV, LANES), F32),
            pltpu.VMEM((group, per * 8 + 1, LANES), F32),
            pltpu.VMEM((group, per * 8 + 1, LANES), F32),
            pltpu.VMEM((2,) + flat, F32),
            pltpu.VMEM((nz, per, ng, LANES), F32),
            pltpu.VMEM((nz, per, ng, LANES), F32),
            pltpu.VMEM((group * rows3, LANES), F32),
            pltpu.VMEM((group, rows3, LANES), F32),
            pltpu.VMEM((2, LEV, LANES), F32),
            pltpu.VMEM((2, LEV, LANES), F32),
            pltpu.VMEM((8, LEV, LANES), F32),
            pltpu.VMEM((16, 2, LEV, LANES), F32),
            dma((9,)),
            dma((2, 2)),
            dma((2, 2)),
            dma((2,)),
            dma((2,)),
            dma((2,)),
            dma((2,)),
            dma((3,)),
            dma((3,)),
            dma((2,)),
            dma((2,)),
        ],
        compiler_params=pltpu.CompilerParams(
            collective_id=0, has_side_effects=True, vmem_limit_bytes=40 * 1024 * 1024
        ),
        name="analysis",
    )(
        block_count,
        *(
            pltpu.with_memory_space_constraint(value, pltpu.HBM)
            for value in (
                obs_values,
                obs_weight,
                obs_box,
                obs_owner,
                diff_x.reshape(flat),
                diff_y.reshape(flat),
                spread_std.reshape(flat),
                land_sea,
                vert_corr,
            )
        ),
    )
    return out.reshape(LEV, 8, LANES)


def solution(mesh):
    in_specs = (
        P(("gx", "gy"), None, None),
        P(("gx", "gy"), None),
        P(("gx", "gy"), None),
        P(("gx", "gy")),
        P(("gx", "gy")),
        P(None, "gx", "gy"),
        P(None, "gx", "gy"),
        P(None, "gx", "gy"),
        P("gx", "gy"),
        P(),
    )
    return jax.shard_map(
        functools.partial(local, mesh.shape["gx"] // 2, mesh.shape["gy"]),
        mesh=mesh,
        in_specs=in_specs,
        out_specs=P(None, "gx", "gy"),
        check_vma=False,
    )
```

```python
import functools

import jax
import jax.numpy as jnp
from jax import lax
from jax.experimental import pallas as pl
from jax.experimental.pallas import tpu as pltpu
from jax.sharding import PartitionSpec as P

MESH = pl.DeviceIdType.MESH
F32 = jnp.float32
BF16 = jnp.bfloat16
LEV = 48
LANES = 128
PASSES = 4
NEAR = 2
CHUNK = 16


def two_terms(x):
    high = x.astype(BF16)
    return high, (x - high.astype(F32)).astype(BF16)


def mul(a, b):
    return jnp.dot(a, b, preferred_element_type=F32)


def mul_terms(a, b):
    a_high, a_low = two_terms(a)
    b_high, b_low = two_terms(b)
    return mul(a_high, b_high) + mul(a_high, b_low) + mul(a_low, b_high)


def lane_of(shape):
    return lax.broadcasted_iota(jnp.int32, shape, len(shape) - 1)


def kernel(
    nz,
    ng,
    count,
    vals_hbm,
    weight_hbm,
    box_hbm,
    owner_hbm,
    dx_hbm,
    dy_hbm,
    sp_hbm,
    land_hbm,
    corr_hbm,
    out_v,
    weight,
    box,
    owner,
    land,
    corr,
    vals,
    raw,
    ext,
    edge,
    pack_s,
    pack_r,
    slab_s,
    slab_r,
    sums_s,
    sums_r,
    by_level,
    part_s,
    part_r,
    tile_s,
    tile_r,
    box_s,
    box_r,
    field,
    face_below,
    local_sem,
    bulk_send,
    bulk_recv,
    pack_send,
    pack_recv,
    slab_send,
    slab_recv,
    all_send,
    all_recv,
    box_send,
    box_recv,
):
    group = 2 * ng
    per = LEV // ng
    rows1 = per * 8
    late = per // 3
    early = per - late
    late8 = late * 8
    rows3 = tile_r.shape[1]
    sent3 = -(-per // 4) * 4
    owners = nz * ng
    depth = group * 8
    gx = lax.axis_index("gx")
    gy = lax.axis_index("gy")
    half = lax.div(gx, nz)
    z = lax.rem(gx, nz)
    me = half * ng + gy

    nx = ng // 4
    y = 2 * lax.div(gy, ng // 2) + half
    x_core = lax.rem(gy, ng // 2)
    chip_x, core = lax.div(x_core, 2), lax.rem(x_core, 2)

    def hops(step, size):
        return min(step, size - step)

    offsets = sorted(
        (
            (oy, ox, oc)
            for oy in range(4)
            for ox in range(nx)
            for oc in range(2)
            if oy or ox or oc
        ),
        key=lambda o: (-hops(o[0], 4) - hops(o[1], nx), o[2], (o[0] + o[1]) % 4, o),
    )
    z_steps = sorted(range(1, nz), key=lambda step: (-hops(step, nz), step))

    def member(offset):
        to_y = lax.rem(y + offset[0], 4)
        to_x = lax.rem(chip_x + offset[1], nx)
        to_core = lax.rem(core + offset[2], 2)
        h = lax.rem(to_y, 2)
        g = lax.div(to_y, 2) * (ng // 2) + 2 * to_x + to_core
        return h * ng + g, (h * nz + z, g)

    def along_z(step):
        target = lax.rem(z + step, nz)
        return target, (half * nz + target, gy)

    east = (lax.rem(gx + 1, 2 * nz), gy)
    west = (lax.rem(gx + 2 * nz - 1, 2 * nz), gy)
    north = (gx, lax.rem(gy + 1, ng))
    south = (gx, lax.rem(gy + ng - 1, ng))

    def remote(src, dst, send, recv, device):
        return pltpu.make_async_remote_copy(
            src_ref=src,
            dst_ref=dst,
            send_sem=send,
            recv_sem=recv,
            device_id=device,
            device_id_type=MESH,
        )

    tile_r[...] = jnp.zeros(tile_r.shape, F32)
    tile_s[...] = jnp.zeros(tile_s.shape, F32)
    loads = [
        pltpu.make_async_copy(owner_hbm, owner, local_sem.at[0]),
        pltpu.make_async_copy(weight_hbm, weight, local_sem.at[1]),
        pltpu.make_async_copy(box_hbm, box, local_sem.at[2]),
        pltpu.make_async_copy(vals_hbm, vals, local_sem.at[3]),
        pltpu.make_async_copy(land_hbm, land, local_sem.at[4]),
        pltpu.make_async_copy(dx_hbm, raw.at[0], local_sem.at[5]),
        pltpu.make_async_copy(dy_hbm, raw.at[1], local_sem.at[6]),
        pltpu.make_async_copy(sp_hbm, raw.at[2], local_sem.at[7]),
        pltpu.make_async_copy(corr_hbm, corr, local_sem.at[8]),
    ]
    for load in loads[:4]:
        load.start()

    barrier = pltpu.get_barrier_semaphore()

    for device in (
        *(member(offset)[1] for offset in offsets),
        *(along_z(step)[1] for step in z_steps),
        east,
        west,
    ):
        pl.semaphore_signal(barrier, inc=1, device_id=device, device_id_type=MESH)
    for load in loads[4:]:
        load.start()

    for load in loads[:4]:
        load.wait()
    weighted = jnp.where(
        lax.broadcasted_iota(jnp.int32, (16, LANES), 0) < count[0], weight[...], 0.0
    )
    boxes = box[...]
    place = (boxes >> 6) * LANES + (boxes & 63)
    target = lax.broadcasted_iota(jnp.int32, (2 * LANES, LANES), 0)
    for j in range(8):
        terms = []
        hots = []
        for parity in range(2):
            b = 2 * j + parity
            value = vals[b].astype(F32) * weighted[b : b + 1, :]
            terms.append(two_terms(value))
            hit = target == place[b : b + 1, :] + 64 * parity
            hots.append(jnp.where(hit, 1.0, 0.0).astype(BF16))
        left = jnp.concatenate(
            [
                jnp.concatenate([terms[0][0], terms[1][0]], axis=1),
                jnp.concatenate([terms[0][1], terms[1][1]], axis=1),
            ],
            axis=0,
        )
        hot = jnp.concatenate(hots, axis=1)
        total = lax.dot_general(left, hot, (((1,), (1,)), ((), ())), preferred_element_type=F32)
        total = total[:LEV] + total[LEV:]
        by_level[0, pl.ds(j, LEV, stride=8), :] = total[:, :LANES]
        by_level[1, pl.ds(j, LEV, stride=8), :] = total[:, LANES:]

    lane1 = lane_of((1, LANES))
    base = lax.rem(me * 8, LANES)
    base_odd = lax.rem(me * 8 + 64, LANES)
    owner_row = jnp.zeros((1, LANES), F32)
    for j in range(8):
        owner_row = jnp.where(lane1 == base + j, owner[2 * j].astype(F32), owner_row)
        owner_row = jnp.where(lane1 == base_odd + j, owner[2 * j + 1].astype(F32), owner_row)
    for h in range(2):
        for g in range(ng):
            low = g * rows1
            sums_s[h * ng + g, late8:rows1, :] = by_level[h, low : low + rows1 - late8, :]
            sums_s[h * ng + g, 0:late8, :] = by_level[h, low + rows1 - late8 : low + rows1, :]
            sums_s[h * ng + g, rows1 : rows1 + 1, :] = owner_row

    for load in loads[4:]:
        load.wait()
    mask = land[...].astype(F32)
    for x in range(8):
        for a in range(3):
            value = raw[a, pl.ds(x, LEV, stride=8), :]
            if a == 2:
                value = value * mask[x : x + 1, :]
            ext[4 + x, a] = value

    lane = lane_of((LEV, LANES))
    for part in range(2):
        to_south = jnp.zeros((LEV, LANES), F32)
        to_north = jnp.zeros((LEV, LANES), F32)
        for r in range(4):
            for a in range(3):
                q = 3 * r + a
                value = ext[4 + 4 * part + r, a]
                if q:
                    value = pltpu.roll(value, 8 * q, 1)
                low = (8 * q + LANES - 4) % LANES
                to_south = jnp.where((lane >= 8 * q) & (lane < 8 * q + 4), value, to_south)
                to_north = jnp.where((lane >= low) & (lane < low + 4), value, to_north)
        pack_s[0, part] = to_south
        pack_s[1, part] = to_north
    packs = [
        remote(pack_s.at[0], pack_r.at[0], pack_send.at[0], pack_recv.at[0], south),
        remote(pack_s.at[1], pack_r.at[1], pack_send.at[1], pack_recv.at[1], north),
    ]
    pl.semaphore_wait(barrier, group + nz)
    for copy in packs:
        copy.start()


    early_rows = pl.ds(late8, rows1 + 1 - late8)
    late_rows = pl.ds(0, late8)
    for k, rows in enumerate((early_rows, late_rows)):
        for offset in offsets:
            index, device = member(offset)
            remote(
                sums_s.at[index, rows],
                sums_r.at[me, rows],
                all_send.at[k],
                all_recv.at[k],
                device,
            ).start()
    sums_r[me] = sums_s[me]

    for copy in packs:
        copy.wait()
    for part in range(2):
        from_north = jnp.where(gy < ng - 1, pack_r[0, part], 0.0)
        from_south = jnp.where(gy > 0, pack_r[1, part], 0.0)
        slab_s[part] = jnp.where((lane & 7) < 4, from_north, from_south)
    slabs = [
        remote(slab_s.at[0], slab_r.at[1], slab_send.at[0], slab_recv.at[0], west),
        remote(slab_s.at[1], slab_r.at[0], slab_send.at[1], slab_recv.at[1], east),
    ]
    for copy in slabs:
        copy.start()
    def rows_to_neighbours(index, low, size):
        return [
            remote(
                ext.at[pl.ds(4 + low, size)],
                ext.at[pl.ds(12 + low, size)],
                bulk_send.at[index, 0],
                bulk_recv.at[index, 0],
                west,
            ),
            remote(
                ext.at[pl.ds(12 - low - size, size)],
                ext.at[pl.ds(4 - low - size, size)],
                bulk_send.at[index, 1],
                bulk_recv.at[index, 1],
                east,
            ),
        ]

    bulk = rows_to_neighbours(0, 0, NEAR)
    for copy in bulk:
        copy.start()

    level = lax.broadcasted_iota(jnp.int32, (LEV, ng * rows3), 0)
    column = lane_of((LEV, ng * rows3))
    from_group = column // rows3
    within = column - from_group * rows3
    chosen = (within < per) & (from_group * per + within == level)
    corr_v = corr[...]
    corr_rows = jnp.dot(
        corr_v,
        jnp.where(chosen, 1.0, 0.0),
        precision=lax.Precision.HIGHEST,
        preferred_element_type=F32,
    )

    for copy in slabs:
        copy.wait()
    outer = (lane < 4) | (lane >= LANES - 4)
    for part in range(4):
        slab = (slab_r[0], slab_s[0], slab_s[1], slab_r[1])[part]
        for r in range(4):
            for a in range(3):
                q = 3 * r + a
                value = pltpu.roll(slab, LANES - 8 * q, 1) if q else slab
                edge[4 * part + r, a] = jnp.where(outer, value, 0.0)

    def wait_bytes(ref, sem, size):
        view = ref.at[pl.ds(0, size)]
        pltpu.make_async_copy(view, view, sem).wait()

    wait_bytes(sums_r.at[:, early_rows], all_recv.at[0], group - 1)
    wide = (depth + LANES - 1) // LANES
    owner_rows = []
    for parity in range(2):
        pieces = []
        for piece in range(wide):
            row = jnp.zeros((1, LANES), F32)
            for source in range(piece * 16, min(group, piece * 16 + 16)):
                start = (source * 8 + 64 * parity) % LANES
                row = jnp.where(
                    (lane1 >= start) & (lane1 < start + 8),
                    sums_r[source, rows1 : rows1 + 1, :],
                    row,
                )
            pieces.append(pltpu.roll(row, 64, 1) if parity else row)
        row = jnp.concatenate(pieces, axis=1) if wide > 1 else pieces[0]
        owner_rows.append(row[:, :depth])
    candidate = lax.broadcasted_iota(jnp.int32, (owners, depth), 0)
    even, odd = (row.astype(jnp.int32) for row in owner_rows)

    def hits(row, shift):
        return jnp.where(row == candidate + shift, 1.0, 0.0).astype(BF16)

    left = jnp.concatenate(
        [
            jnp.concatenate([hits(even, 0), hits(odd, 0)], axis=1),
            jnp.concatenate([hits(odd, owners), hits(even, owners)], axis=1),
        ],
        axis=0,
    )
    lower = lane_of((owners, LANES)) < 64

    def add_by_owner(k, first_level, levels, first_row):
        columns = []
        for t in range(levels):
            low = first_row + 8 * t
            value = sums_r[:, low : low + 8, :].reshape(depth, LANES)
            columns.append(jnp.concatenate([value, pltpu.roll(value, 64, 1)], axis=0))
        stack_high, stack_low = two_terms(jnp.concatenate(columns, axis=1))
        by_owner = mul(left, stack_high) + mul(left, stack_low)
        for t in range(levels):
            cut = by_owner[:, t * LANES : (t + 1) * LANES]
            part_s[:, first_level + t] = jnp.where(
                lower, cut[:owners], cut[owners:]
            ).reshape(nz, ng, LANES)
        for step in z_steps:
            index, device = along_z(step)
            chosen_levels = pl.ds(first_level, levels)
            remote(
                part_s.at[index, chosen_levels],
                part_r.at[z, chosen_levels],
                all_send.at[2 + k],
                all_recv.at[2 + k],
                device,
            ).start()

    add_by_owner(0, 0, early, late8)
    wait_bytes(sums_r.at[:, late_rows], all_recv.at[1], group - 1)
    add_by_owner(1, early, late, 0)
    part_r[z] = part_s[z]

    for copy in bulk:
        copy.wait()

    def faces(x, _):
        here, beyond = ext[x, 2], edge[x, 2]
        last = lane == LANES - 1
        turned, turned_beyond = pltpu.roll(here, LANES - 1, 1), pltpu.roll(beyond, LANES - 1, 1)
        ext[x, 0] = jnp.where(here * ext[x + 1, 2] > 0.0, ext[x, 0], 0.0)
        edge[x, 0] = jnp.where(beyond * edge[x + 1, 2] > 0.0, edge[x, 0], 0.0)
        upper = jnp.where(last, turned_beyond, turned)
        upper_beyond = jnp.where(last, turned, turned_beyond)
        north_face = jnp.where(here * upper > 0.0, ext[x, 1], 0.0)
        north_face_beyond = jnp.where(beyond * upper_beyond > 0.0, edge[x, 1], 0.0)
        turned, turned_beyond = pltpu.roll(north_face, 1, 1), pltpu.roll(north_face_beyond, 1, 1)
        ext[x, 1] = north_face
        edge[x, 1] = north_face_beyond
        face_below[x, 0] = jnp.where(lane == 0, turned_beyond, turned)
        face_below[x, 1] = jnp.where(lane == 0, turned, turned_beyond)
        return _

    lax.fori_loop(4 - NEAR, 11 + NEAR, faces, 0)

    parts = [
        (part_r.at[:, pl.ds(0, early)], 2),
        (part_r.at[:, pl.ds(early, late)], 3),
    ]
    for ref, k in parts:
        wait_bytes(ref, all_recv.at[k], nz - 1)
    row = lax.broadcasted_iota(jnp.int32, (ng, LANES), 0)
    box_column = lane_of((ng, LANES)) & 15
    low_boxes = lane_of((ng, LANES)) < 64
    for t in range(per):
        value = part_r[0, t]
        for source in range(1, nz):
            value = value + part_r[source, t]
        below = jnp.where(row == 0, 0.0, pltpu.roll(value, 1, 0))
        above = jnp.where(row == ng - 1, 0.0, pltpu.roll(value, ng - 1, 0))
        near = jnp.where(box_column == 15, below, above)
        other, other_near = pltpu.roll(value, 64, 1), pltpu.roll(near, 64, 1)
        tile_s[pl.ds(t, ng, stride=rows3), :] = jnp.where(low_boxes, value, other_near)
        tile_s[pl.ds(ng * rows3 + t, ng, stride=rows3), :] = jnp.where(low_boxes, other, near)

    first_rows = pl.ds(0, sent3)
    for offset in offsets:
        index, device = member(offset)
        start = pl.multiple_of(index * rows3, 8)
        remote(
            tile_s.at[pl.ds(start, sent3)],
            tile_r.at[me, first_rows],
            all_send.at[4],
            all_recv.at[4],
            device,
        ).start()
    far = rows_to_neighbours(1, NEAR, 4 - NEAR)
    for copy in far:
        copy.start()
    tile_r[me] = tile_s[pl.ds(pl.multiple_of(me * rows3, 8), rows3), :]

    wait_bytes(tile_r.at[:, first_rows], all_recv.at[4], group - 1)
    arrived = jnp.concatenate(
        [tile_r[h * ng : (h + 1) * ng].reshape(ng * rows3, LANES) for h in range(2)], axis=1
    )
    mixed = mul_terms(corr_rows, arrived)
    for h in range(2):
        box_s[h] = mixed[:, h * LANES : (h + 1) * LANES]
    borders = [
        remote(box_s.at[0], box_r.at[1], box_send.at[0], box_recv.at[0], west),
        remote(box_s.at[1], box_r.at[0], box_send.at[1], box_recv.at[1], east),
    ]
    for copy in borders:
        copy.start()
    for copy in far:
        copy.wait()
    lax.fori_loop(0, 4 - NEAR, faces, 0)
    lax.fori_loop(11 + NEAR, 15, faces, 0)
    for copy in borders:
        copy.wait()

    lane8 = lane_of((CHUNK, LANES))
    first, last = lane8 == 0, lane8 == LANES - 1

    def advance(step, _):
        rows = pl.ds(pl.multiple_of(step * CHUNK, 8), CHUNK)
        inner, outside = [], []
        for part in range(4):
            source = (box_r.at[0], box_s.at[0], box_s.at[1], box_r.at[1])[part]
            value = source[rows, :]
            for r in range(4):
                x = 4 * part + r
                at_inner = 16 * r + (lane8 >> 3)
                at_outside = jnp.where(lane8 < 64, 64 + 16 * r, 64 + 16 * r + 15)
                inner.append(ext[x, 2, rows, :] * jnp.take_along_axis(value, at_inner, axis=1))
                outside.append(
                    edge[x, 2, rows, :] * jnp.take_along_axis(value, at_outside, axis=1)
                )
        for turn in range(PASSES):
            low, high = 1 + turn, 15 - turn
            final = turn == PASSES - 1
            turned = {}
            for x in range(low, high):
                turned[x] = [
                    pltpu.roll(value[x], shift, 1)
                    for shift in (LANES - 1, 1)
                    for value in (inner, outside)
                ]
            flow = {}
            for x in range(low - 1, high):
                flow[x] = ext[x, 0, rows, :] * (inner[x + 1] - inner[x])
            new_inner, new_outside = list(inner), list(outside)
            for x in range(low, high):
                here = inner[x]
                above, above_beyond, below, below_beyond = turned[x]
                up = ext[x, 1, rows, :] * (jnp.where(last, above_beyond, above) - here)
                down = face_below[x, 0, rows, :] * (jnp.where(first, below_beyond, below) - here)
                new_inner[x] = here + (flow[x] - flow[x - 1]) + (up + down)
            if not final:
                for x in range(low - 1, high):
                    flow[x] = edge[x, 0, rows, :] * (outside[x + 1] - outside[x])
                for x in range(low, high):
                    here = outside[x]
                    above, above_beyond, below, below_beyond = turned[x]
                    up = edge[x, 1, rows, :] * (jnp.where(last, above, above_beyond) - here)
                    down = face_below[x, 1, rows, :] * (
                        jnp.where(first, below, below_beyond) - here
                    )
                    new_outside[x] = here + (flow[x] - flow[x - 1]) + (up + down)
            inner, outside = new_inner, new_outside
        for x in range(8):
            field[x, rows, :] = inner[4 + x]
        return _

    lax.fori_loop(0, LEV // CHUNK, advance, 0)

    whole = jnp.concatenate([field[x] for x in range(8)], axis=1)
    result = mul_terms(corr_v, whole)
    for x in range(8):
        out_v[pl.ds(x, LEV, stride=8), :] = ext[4 + x, 2] * result[:, x * LANES : (x + 1) * LANES]

    wait_bytes(sums_r.at[:, early_rows], all_send.at[0], group - 1)
    wait_bytes(sums_r.at[:, late_rows], all_send.at[1], group - 1)
    for ref, k in parts:
        wait_bytes(ref, all_send.at[k], nz - 1)
    wait_bytes(tile_r.at[:, first_rows], all_send.at[4], group - 1)


def local(
    nz,
    ng,
    obs_values,
    obs_weight,
    obs_box,
    obs_owner,
    block_count,
    diff_x,
    diff_y,
    spread_std,
    land_sea,
    vert_corr,
):
    group = 2 * ng
    per = LEV // ng
    rows3 = -(-per // 8) * 8
    hbm = pl.BlockSpec(memory_space=pltpu.HBM)
    dma = pltpu.SemaphoreType.DMA
    flat = (LEV * 8, LANES)
    out = pl.pallas_call(
        functools.partial(kernel, nz, ng),
        out_shape=jax.ShapeDtypeStruct(flat, F32),
        in_specs=[pl.BlockSpec(memory_space=pltpu.SMEM)] + [hbm] * 9,
        out_specs=pl.BlockSpec(memory_space=pltpu.VMEM),
        scratch_shapes=[
            pltpu.VMEM((16, LANES), F32),
            pltpu.VMEM((16, LANES), jnp.int32),
            pltpu.SMEM((16,), jnp.int32),
            pltpu.VMEM((8, LANES), jnp.int32),
            pltpu.VMEM((LEV, LEV), F32),
            pltpu.VMEM((16, LEV, LANES), BF16),
            pltpu.VMEM((3,) + flat, F32),
            pltpu.VMEM((16, 3, LEV, LANES), F32),
            pltpu.VMEM((16, 3, LEV, LANES), F32),
            pltpu.VMEM((2, 2, LEV, LANES), F32),
            pltpu.VMEM((2, 2, LEV, LANES), F32),
            pltpu.VMEM((2, LEV, LANES), F32),
            pltpu.VMEM((2, LEV, LANES), F32),
            pltpu.VMEM((group, per * 8 + 1, LANES), F32),
            pltpu.VMEM((group, per * 8 + 1, LANES), F32),
            pltpu.VMEM((2,) + flat, F32),
            pltpu.VMEM((nz, per, ng, LANES), F32),
            pltpu.VMEM((nz, per, ng, LANES), F32),
            pltpu.VMEM((group * rows3, LANES), F32),
            pltpu.VMEM((group, rows3, LANES), F32),
            pltpu.VMEM((2, LEV, LANES), F32),
            pltpu.VMEM((2, LEV, LANES), F32),
            pltpu.VMEM((8, LEV, LANES), F32),
            pltpu.VMEM((16, 2, LEV, LANES), F32),
            dma((9,)),
            dma((2, 2)),
            dma((2, 2)),
            dma((2,)),
            dma((2,)),
            dma((2,)),
            dma((2,)),
            dma((5,)),
            dma((5,)),
            dma((2,)),
            dma((2,)),
        ],
        compiler_params=pltpu.CompilerParams(
            collective_id=0, has_side_effects=True, vmem_limit_bytes=40 * 1024 * 1024
        ),
        name="analysis",
    )(
        block_count,
        *(
            pltpu.with_memory_space_constraint(value, pltpu.HBM)
            for value in (
                obs_values,
                obs_weight,
                obs_box,
                obs_owner,
                diff_x.reshape(flat),
                diff_y.reshape(flat),
                spread_std.reshape(flat),
                land_sea,
                vert_corr,
            )
        ),
    )
    return out.reshape(LEV, 8, LANES)


def solution(mesh):
    in_specs = (
        P(("gx", "gy"), None, None),
        P(("gx", "gy"), None),
        P(("gx", "gy"), None),
        P(("gx", "gy")),
        P(("gx", "gy")),
        P(None, "gx", "gy"),
        P(None, "gx", "gy"),
        P(None, "gx", "gy"),
        P("gx", "gy"),
        P(),
    )
    return jax.shard_map(
        functools.partial(local, mesh.shape["gx"] // 2, mesh.shape["gy"]),
        mesh=mesh,
        in_specs=in_specs,
        out_specs=P(None, "gx", "gy"),
        check_vma=False,
    )
```

```python
import functools

import jax
import jax.numpy as jnp
from jax import lax
from jax.experimental import pallas as pl
from jax.experimental.pallas import tpu as pltpu
from jax.sharding import PartitionSpec as P

MESH = pl.DeviceIdType.MESH
F32 = jnp.float32
BF16 = jnp.bfloat16
LEV = 48
LANES = 128
PASSES = 4
NEAR = 2
CHUNK = 16
CHUNK_END = 24


def two_terms(x):
    high = x.astype(BF16)
    return high, (x - high.astype(F32)).astype(BF16)


def mul(a, b):
    return jnp.dot(a, b, preferred_element_type=F32)


def mul_terms(a, b):
    a_high, a_low = two_terms(a)
    b_high, b_low = two_terms(b)
    return mul(a_high, b_high) + mul(a_high, b_low) + mul(a_low, b_high)


def lane_of(shape):
    return lax.broadcasted_iota(jnp.int32, shape, len(shape) - 1)


def kernel(
    nz,
    ng,
    count,
    vals_hbm,
    weight_hbm,
    box_hbm,
    owner_hbm,
    dx_hbm,
    dy_hbm,
    sp_hbm,
    land_hbm,
    corr_hbm,
    out_v,
    weight,
    box,
    owner,
    land,
    corr,
    vals,
    raw,
    ext,
    edge,
    pack_s,
    pack_r,
    slab_s,
    slab_r,
    sums_s,
    sums_r,
    by_level,
    part_s,
    part_r,
    tile_s,
    tile_r,
    box_s,
    box_r,
    field,
    face_below,
    ready,
    local_sem,
    bulk_send,
    bulk_recv,
    pack_send,
    pack_recv,
    slab_send,
    slab_recv,
    all_send,
    all_recv,
    box_send,
    box_recv,
):
    group = 2 * ng
    per = LEV // ng
    rows1 = per * 8
    late = per // 3
    early = per - late
    late8 = late * 8
    rows3 = tile_r.shape[1]
    sent3 = -(-per // 4) * 4
    owners = nz * ng
    depth = group * 8
    gx = lax.axis_index("gx")
    gy = lax.axis_index("gy")
    half = lax.div(gx, nz)
    z = lax.rem(gx, nz)
    me = half * ng + gy

    nx = ng // 4
    y = 2 * lax.div(gy, ng // 2) + half
    x_core = lax.rem(gy, ng // 2)
    chip_x, core = lax.div(x_core, 2), lax.rem(x_core, 2)

    def hops(step, size):
        return min(step, size - step)

    offsets = sorted(
        (
            (oy, ox, oc)
            for oy in range(4)
            for ox in range(nx)
            for oc in range(2)
            if oy or ox or oc
        ),
        key=lambda o: (-hops(o[0], 4) - hops(o[1], nx), o[2], (o[0] + o[1]) % 4, o),
    )
    z_steps = sorted(range(1, nz), key=lambda step: (-hops(step, nz), step))

    def member(offset):
        to_y = lax.rem(y + offset[0], 4)
        to_x = lax.rem(chip_x + offset[1], nx)
        to_core = lax.rem(core + offset[2], 2)
        h = lax.rem(to_y, 2)
        g = lax.div(to_y, 2) * (ng // 2) + 2 * to_x + to_core
        return h * ng + g, (h * nz + z, g)

    def along_z(step):
        target = lax.rem(z + step, nz)
        return target, (half * nz + target, gy)

    east = (lax.rem(gx + 1, 2 * nz), gy)
    west = (lax.rem(gx + 2 * nz - 1, 2 * nz), gy)
    north = (gx, lax.rem(gy + 1, ng))
    south = (gx, lax.rem(gy + ng - 1, ng))

    def remote(src, dst, send, recv, device):
        return pltpu.make_async_remote_copy(
            src_ref=src,
            dst_ref=dst,
            send_sem=send,
            recv_sem=recv,
            device_id=device,
            device_id_type=MESH,
        )

    tile_r[...] = jnp.zeros(tile_r.shape, F32)
    tile_s[...] = jnp.zeros(tile_s.shape, F32)
    loads = [
        pltpu.make_async_copy(owner_hbm, owner, local_sem.at[0]),
        pltpu.make_async_copy(weight_hbm, weight, local_sem.at[1]),
        pltpu.make_async_copy(box_hbm, box, local_sem.at[2]),
        pltpu.make_async_copy(vals_hbm, vals, local_sem.at[3]),
        pltpu.make_async_copy(land_hbm, land, local_sem.at[4]),
        pltpu.make_async_copy(dx_hbm, raw.at[0], local_sem.at[5]),
        pltpu.make_async_copy(dy_hbm, raw.at[1], local_sem.at[6]),
        pltpu.make_async_copy(sp_hbm, raw.at[2], local_sem.at[7]),
        pltpu.make_async_copy(corr_hbm, corr, local_sem.at[8]),
    ]
    for load in loads[:4]:
        load.start()

    barrier = pltpu.get_barrier_semaphore()

    for device in (
        *(member(offset)[1] for offset in offsets),
        *(along_z(step)[1] for step in z_steps),
        east,
        west,
    ):
        pl.semaphore_signal(barrier, inc=1, device_id=device, device_id_type=MESH)
    for load in loads[4:]:
        load.start()

    for load in loads[:4]:
        load.wait()
    weighted = jnp.where(
        lax.broadcasted_iota(jnp.int32, (16, LANES), 0) < count[0], weight[...], 0.0
    )
    boxes = box[...]
    place = (boxes >> 6) * LANES + (boxes & 63)
    target = lax.broadcasted_iota(jnp.int32, (2 * LANES, LANES), 0)
    for j in range(8):
        terms = []
        hots = []
        for parity in range(2):
            b = 2 * j + parity
            value = vals[b].astype(F32) * weighted[b : b + 1, :]
            terms.append(two_terms(value))
            hit = target == place[b : b + 1, :] + 64 * parity
            hots.append(jnp.where(hit, 1.0, 0.0).astype(BF16))
        left = jnp.concatenate(
            [
                jnp.concatenate([terms[0][0], terms[1][0]], axis=1),
                jnp.concatenate([terms[0][1], terms[1][1]], axis=1),
            ],
            axis=0,
        )
        hot = jnp.concatenate(hots, axis=1)
        total = lax.dot_general(left, hot, (((1,), (1,)), ((), ())), preferred_element_type=F32)
        total = total[:LEV] + total[LEV:]
        by_level[0, pl.ds(j, LEV, stride=8), :] = total[:, :LANES]
        by_level[1, pl.ds(j, LEV, stride=8), :] = total[:, LANES:]

    lane1 = lane_of((1, LANES))
    base = lax.rem(me * 8, LANES)
    base_odd = lax.rem(me * 8 + 64, LANES)
    owner_row = jnp.zeros((1, LANES), F32)
    for j in range(8):
        owner_row = jnp.where(lane1 == base + j, owner[2 * j].astype(F32), owner_row)
        owner_row = jnp.where(lane1 == base_odd + j, owner[2 * j + 1].astype(F32), owner_row)
    for h in range(2):
        for g in range(ng):
            low = g * rows1
            sums_s[h * ng + g, late8:rows1, :] = by_level[h, low : low + rows1 - late8, :]
            sums_s[h * ng + g, 0:late8, :] = by_level[h, low + rows1 - late8 : low + rows1, :]
            sums_s[h * ng + g, rows1 : rows1 + 1, :] = owner_row

    for load in loads[4:]:
        load.wait()
    mask = land[...].astype(F32)
    for x in range(8):
        for a in range(3):
            value = raw[a, pl.ds(x, LEV, stride=8), :]
            if a == 2:
                value = value * mask[x : x + 1, :]
            ext[4 + x, a] = value

    lane = lane_of((LEV, LANES))
    for part in range(2):
        to_south = jnp.zeros((LEV, LANES), F32)
        to_north = jnp.zeros((LEV, LANES), F32)
        for r in range(4):
            for a in range(3):
                q = 3 * r + a
                value = ext[4 + 4 * part + r, a]
                if q:
                    value = pltpu.roll(value, 8 * q, 1)
                low = (8 * q + LANES - 4) % LANES
                to_south = jnp.where((lane >= 8 * q) & (lane < 8 * q + 4), value, to_south)
                to_north = jnp.where((lane >= low) & (lane < low + 4), value, to_north)
        pack_s[0, part] = to_south
        pack_s[1, part] = to_north
    packs = [
        remote(pack_s.at[0], pack_r.at[0], pack_send.at[0], pack_recv.at[0], south),
        remote(pack_s.at[1], pack_r.at[1], pack_send.at[1], pack_recv.at[1], north),
    ]
    pl.semaphore_wait(barrier, group + nz)
    for copy in packs:
        copy.start()


    early_rows = pl.ds(late8, rows1 + 1 - late8)
    late_rows = pl.ds(0, late8)
    for k, rows in enumerate((early_rows, late_rows)):
        for offset in offsets:
            index, device = member(offset)
            remote(
                sums_s.at[index, rows],
                sums_r.at[me, rows],
                all_send.at[k],
                all_recv.at[k],
                device,
            ).start()
    sums_r[me] = sums_s[me]

    for copy in packs:
        copy.wait()
    for part in range(2):
        from_north = jnp.where(gy < ng - 1, pack_r[0, part], 0.0)
        from_south = jnp.where(gy > 0, pack_r[1, part], 0.0)
        slab_s[part] = jnp.where((lane & 7) < 4, from_north, from_south)
    slabs = [
        remote(slab_s.at[0], slab_r.at[1], slab_send.at[0], slab_recv.at[0], west),
        remote(slab_s.at[1], slab_r.at[0], slab_send.at[1], slab_recv.at[1], east),
    ]
    for copy in slabs:
        copy.start()
    def rows_to_neighbours(index, low, size):
        return [
            remote(
                ext.at[pl.ds(4 + low, size)],
                ext.at[pl.ds(12 + low, size)],
                bulk_send.at[index, 0],
                bulk_recv.at[index, 0],
                west,
            ),
            remote(
                ext.at[pl.ds(12 - low - size, size)],
                ext.at[pl.ds(4 - low - size, size)],
                bulk_send.at[index, 1],
                bulk_recv.at[index, 1],
                east,
            ),
        ]

    bulk = rows_to_neighbours(0, 0, NEAR)
    for copy in bulk:
        copy.start()

    level = lax.broadcasted_iota(jnp.int32, (LEV, ng * rows3), 0)
    column = lane_of((LEV, ng * rows3))
    from_group = column // rows3
    within = column - from_group * rows3
    chosen = (within < per) & (from_group * per + within == level)
    corr_v = corr[...]
    corr_rows = jnp.dot(
        corr_v,
        jnp.where(chosen, 1.0, 0.0),
        precision=lax.Precision.HIGHEST,
        preferred_element_type=F32,
    )

    for copy in slabs:
        copy.wait()
    outer = (lane < 4) | (lane >= LANES - 4)
    for part in range(4):
        slab = (slab_r[0], slab_s[0], slab_s[1], slab_r[1])[part]
        for r in range(4):
            for a in range(3):
                q = 3 * r + a
                value = pltpu.roll(slab, LANES - 8 * q, 1) if q else slab
                edge[4 * part + r, a] = jnp.where(outer, value, 0.0)

    def wait_bytes(ref, sem, size):
        view = ref.at[pl.ds(0, size)]
        pltpu.make_async_copy(view, view, sem).wait()

    wait_bytes(sums_r.at[:, early_rows], all_recv.at[0], group - 1)
    wide = (depth + LANES - 1) // LANES
    owner_rows = []
    for parity in range(2):
        pieces = []
        for piece in range(wide):
            row = jnp.zeros((1, LANES), F32)
            for source in range(piece * 16, min(group, piece * 16 + 16)):
                start = (source * 8 + 64 * parity) % LANES
                row = jnp.where(
                    (lane1 >= start) & (lane1 < start + 8),
                    sums_r[source, rows1 : rows1 + 1, :],
                    row,
                )
            pieces.append(pltpu.roll(row, 64, 1) if parity else row)
        row = jnp.concatenate(pieces, axis=1) if wide > 1 else pieces[0]
        owner_rows.append(row[:, :depth])
    candidate = lax.broadcasted_iota(jnp.int32, (owners, depth), 0)
    even, odd = (row.astype(jnp.int32) for row in owner_rows)

    def hits(row, shift):
        return jnp.where(row == candidate + shift, 1.0, 0.0).astype(BF16)

    left = jnp.concatenate(
        [
            jnp.concatenate([hits(even, 0), hits(odd, 0)], axis=1),
            jnp.concatenate([hits(odd, owners), hits(even, owners)], axis=1),
        ],
        axis=0,
    )
    lower = lane_of((owners, LANES)) < 64

    def add_by_owner(k, first_level, levels, first_row):
        columns = []
        for t in range(levels):
            low = first_row + 8 * t
            value = sums_r[:, low : low + 8, :].reshape(depth, LANES)
            columns.append(jnp.concatenate([value, pltpu.roll(value, 64, 1)], axis=0))
        stack_high, stack_low = two_terms(jnp.concatenate(columns, axis=1))
        by_owner = mul(left, stack_high) + mul(left, stack_low)
        for t in range(levels):
            cut = by_owner[:, t * LANES : (t + 1) * LANES]
            part_s[:, first_level + t] = jnp.where(
                lower, cut[:owners], cut[owners:]
            ).reshape(nz, ng, LANES)
        for step in z_steps:
            index, device = along_z(step)
            chosen_levels = pl.ds(first_level, levels)
            remote(
                part_s.at[index, chosen_levels],
                part_r.at[z, chosen_levels],
                all_send.at[2 + k],
                all_recv.at[2 + k],
                device,
            ).start()

    add_by_owner(0, 0, early, late8)
    wait_bytes(sums_r.at[:, late_rows], all_recv.at[1], group - 1)
    add_by_owner(1, early, late, 0)
    part_r[z] = part_s[z]

    for copy in bulk:
        copy.wait()

    def faces(x, _):
        here, beyond = ext[x, 2], edge[x, 2]
        last = lane == LANES - 1
        turned, turned_beyond = pltpu.roll(here, LANES - 1, 1), pltpu.roll(beyond, LANES - 1, 1)
        ext[x, 0] = jnp.where(here * ext[x + 1, 2] > 0.0, ext[x, 0], 0.0)
        edge[x, 0] = jnp.where(beyond * edge[x + 1, 2] > 0.0, edge[x, 0], 0.0)
        upper = jnp.where(last, turned_beyond, turned)
        upper_beyond = jnp.where(last, turned, turned_beyond)
        north_face = jnp.where(here * upper > 0.0, ext[x, 1], 0.0)
        north_face_beyond = jnp.where(beyond * upper_beyond > 0.0, edge[x, 1], 0.0)
        turned, turned_beyond = pltpu.roll(north_face, 1, 1), pltpu.roll(north_face_beyond, 1, 1)
        ext[x, 1] = north_face
        edge[x, 1] = north_face_beyond
        face_below[x, 0] = jnp.where(lane == 0, turned_beyond, turned)
        face_below[x, 1] = jnp.where(lane == 0, turned, turned_beyond)
        return _

    lax.fori_loop(4 - NEAR, 11 + NEAR, faces, 0)

    parts = [
        (part_r.at[:, pl.ds(0, early)], 2),
        (part_r.at[:, pl.ds(early, late)], 3),
    ]
    for ref, k in parts:
        wait_bytes(ref, all_recv.at[k], nz - 1)
    row = lax.broadcasted_iota(jnp.int32, (ng, LANES), 0)
    box_column = lane_of((ng, LANES)) & 15
    low_boxes = lane_of((ng, LANES)) < 64
    for t in range(per):
        value = part_r[0, t]
        for source in range(1, nz):
            value = value + part_r[source, t]
        below = jnp.where(row == 0, 0.0, pltpu.roll(value, 1, 0))
        above = jnp.where(row == ng - 1, 0.0, pltpu.roll(value, ng - 1, 0))
        near = jnp.where(box_column == 15, below, above)
        other, other_near = pltpu.roll(value, 64, 1), pltpu.roll(near, 64, 1)
        tile_s[pl.ds(t, ng, stride=rows3), :] = jnp.where(low_boxes, value, other_near)
        tile_s[pl.ds(ng * rows3 + t, ng, stride=rows3), :] = jnp.where(low_boxes, other, near)

    first_rows = pl.ds(0, sent3)
    for offset in offsets:
        index, device = member(offset)
        start = pl.multiple_of(index * rows3, 8)
        remote(
            tile_s.at[pl.ds(start, sent3)],
            tile_r.at[me, first_rows],
            all_send.at[4],
            all_recv.at[4],
            device,
        ).start()
    far = rows_to_neighbours(1, NEAR, 4 - NEAR)
    for copy in far:
        copy.start()
    tile_r[me] = tile_s[pl.ds(pl.multiple_of(me * rows3, 8), rows3), :]

    wait_bytes(tile_r.at[:, first_rows], all_recv.at[4], group - 1)
    arrived = jnp.concatenate(
        [tile_r[h * ng : (h + 1) * ng].reshape(ng * rows3, LANES) for h in range(2)], axis=1
    )
    mixed = mul_terms(corr_rows, arrived)
    for h in range(2):
        box_s[h] = mixed[:, h * LANES : (h + 1) * LANES]
    borders = [
        remote(box_s.at[0], box_r.at[1], box_send.at[0], box_recv.at[0], west),
        remote(box_s.at[1], box_r.at[0], box_send.at[1], box_recv.at[1], east),
    ]
    for copy in borders:
        copy.start()

    def levels_of(step, size):
        rows = pl.ds(pl.multiple_of(step * size, 8), size)
        lanes = lane_of((size, LANES))
        first, last = lanes == 0, lanes == LANES - 1

        def forced(part, source):
            value = source[rows, :]
            made = {}
            for r in range(4):
                x = 4 * part + r
                at_inner = 16 * r + (lanes >> 3)
                at_outside = jnp.where(lanes < 64, 64 + 16 * r, 64 + 16 * r + 15)
                made[x] = (
                    ext[x, 2, rows, :] * jnp.take_along_axis(value, at_inner, axis=1),
                    edge[x, 2, rows, :] * jnp.take_along_axis(value, at_outside, axis=1),
                )
            return made

        def passed(turn, chosen, state):
            needed = sorted({x - 1 for x in chosen} | set(chosen))
            turned = {
                x: [pltpu.roll(state[x][k], shift, 1) for shift in (LANES - 1, 1) for k in range(2)]
                for x in chosen
            }
            result = {x: [None, None] for x in chosen}
            for k, faces_of in enumerate((ext, edge)):
                if k and turn == PASSES - 1:
                    break
                flow = {
                    x: faces_of[x, 0, rows, :] * (state[x + 1][k] - state[x][k]) for x in needed
                }
                for x in chosen:
                    here = state[x][k]
                    above, below = turned[x][:2], turned[x][2:]
                    up = faces_of[x, 1, rows, :] * (
                        jnp.where(last, above[1 - k], above[k]) - here
                    )
                    down = face_below[x, k, rows, :] * (
                        jnp.where(first, below[1 - k], below[k]) - here
                    )
                    result[x][k] = here + (flow[x] - flow[x - 1]) + (up + down)
            return result

        return rows, forced, passed

    def begin(step, _):
        rows, forced, passed = levels_of(step, CHUNK)
        state = {**forced(1, box_s.at[0]), **forced(2, box_s.at[1])}
        for turn in range(PASSES):
            for x in state:
                for k in range(2):
                    ready[turn, x - 4, k, rows, :] = state[x][k]
            if turn < PASSES - 1:
                state = passed(turn, range(5 + turn, 11 - turn), state)
        return _

    def finish(step, _):
        rows, forced, passed = levels_of(step, CHUNK_END)

        def known(turn):
            return {
                x: [ready[turn, x - 4, k, rows, :] for k in range(2)]
                for x in range(4 + turn, 12 - turn)
            }

        state = {**forced(0, box_r.at[0]), **known(0), **forced(3, box_r.at[1])}
        for turn in range(PASSES):
            chosen = [
                x
                for x in range(1 + turn, 15 - turn)
                if turn == PASSES - 1 or not 5 + turn <= x < 11 - turn
            ]
            new = passed(turn, chosen, state)
            state = new if turn == PASSES - 1 else {**new, **known(turn + 1)}
        for x in range(8):
            field[x, rows, :] = state[4 + x][0]
        return _

    lax.fori_loop(0, LEV // CHUNK, begin, 0)
    for copy in far:
        copy.wait()
    lax.fori_loop(0, 4 - NEAR, faces, 0)
    lax.fori_loop(11 + NEAR, 15, faces, 0)
    for copy in borders:
        copy.wait()
    lax.fori_loop(0, LEV // CHUNK_END, finish, 0)

    whole = jnp.concatenate([field[x] for x in range(8)], axis=1)
    result = mul_terms(corr_v, whole)
    for x in range(8):
        out_v[pl.ds(x, LEV, stride=8), :] = ext[4 + x, 2] * result[:, x * LANES : (x + 1) * LANES]

    wait_bytes(sums_r.at[:, early_rows], all_send.at[0], group - 1)
    wait_bytes(sums_r.at[:, late_rows], all_send.at[1], group - 1)
    for ref, k in parts:
        wait_bytes(ref, all_send.at[k], nz - 1)
    wait_bytes(tile_r.at[:, first_rows], all_send.at[4], group - 1)


def local(
    nz,
    ng,
    obs_values,
    obs_weight,
    obs_box,
    obs_owner,
    block_count,
    diff_x,
    diff_y,
    spread_std,
    land_sea,
    vert_corr,
):
    group = 2 * ng
    per = LEV // ng
    rows3 = -(-per // 8) * 8
    hbm = pl.BlockSpec(memory_space=pltpu.HBM)
    dma = pltpu.SemaphoreType.DMA
    flat = (LEV * 8, LANES)
    out = pl.pallas_call(
        functools.partial(kernel, nz, ng),
        out_shape=jax.ShapeDtypeStruct(flat, F32),
        in_specs=[pl.BlockSpec(memory_space=pltpu.SMEM)] + [hbm] * 9,
        out_specs=pl.BlockSpec(memory_space=pltpu.VMEM),
        scratch_shapes=[
            pltpu.VMEM((16, LANES), F32),
            pltpu.VMEM((16, LANES), jnp.int32),
            pltpu.SMEM((16,), jnp.int32),
            pltpu.VMEM((8, LANES), jnp.int32),
            pltpu.VMEM((LEV, LEV), F32),
            pltpu.VMEM((16, LEV, LANES), BF16),
            pltpu.VMEM((3,) + flat, F32),
            pltpu.VMEM((16, 3, LEV, LANES), F32),
            pltpu.VMEM((16, 3, LEV, LANES), F32),
            pltpu.VMEM((2, 2, LEV, LANES), F32),
            pltpu.VMEM((2, 2, LEV, LANES), F32),
            pltpu.VMEM((2, LEV, LANES), F32),
            pltpu.VMEM((2, LEV, LANES), F32),
            pltpu.VMEM((group, per * 8 + 1, LANES), F32),
            pltpu.VMEM((group, per * 8 + 1, LANES), F32),
            pltpu.VMEM((2,) + flat, F32),
            pltpu.VMEM((nz, per, ng, LANES), F32),
            pltpu.VMEM((nz, per, ng, LANES), F32),
            pltpu.VMEM((group * rows3, LANES), F32),
            pltpu.VMEM((group, rows3, LANES), F32),
            pltpu.VMEM((2, LEV, LANES), F32),
            pltpu.VMEM((2, LEV, LANES), F32),
            pltpu.VMEM((8, LEV, LANES), F32),
            pltpu.VMEM((16, 2, LEV, LANES), F32),
            pltpu.VMEM((PASSES, 8, 2, LEV, LANES), F32),
            dma((9,)),
            dma((2, 2)),
            dma((2, 2)),
            dma((2,)),
            dma((2,)),
            dma((2,)),
            dma((2,)),
            dma((5,)),
            dma((5,)),
            dma((2,)),
            dma((2,)),
        ],
        compiler_params=pltpu.CompilerParams(
            collective_id=0, has_side_effects=True, vmem_limit_bytes=40 * 1024 * 1024
        ),
        name="analysis",
    )(
        block_count,
        *(
            pltpu.with_memory_space_constraint(value, pltpu.HBM)
            for value in (
                obs_values,
                obs_weight,
                obs_box,
                obs_owner,
                diff_x.reshape(flat),
                diff_y.reshape(flat),
                spread_std.reshape(flat),
                land_sea,
                vert_corr,
            )
        ),
    )
    return out.reshape(LEV, 8, LANES)


def solution(mesh):
    in_specs = (
        P(("gx", "gy"), None, None),
        P(("gx", "gy"), None),
        P(("gx", "gy"), None),
        P(("gx", "gy")),
        P(("gx", "gy")),
        P(None, "gx", "gy"),
        P(None, "gx", "gy"),
        P(None, "gx", "gy"),
        P("gx", "gy"),
        P(),
    )
    return jax.shard_map(
        functools.partial(local, mesh.shape["gx"] // 2, mesh.shape["gy"]),
        mesh=mesh,
        in_specs=in_specs,
        out_specs=P(None, "gx", "gy"),
        check_vma=False,
    )
```

```python
import functools

import jax
import jax.numpy as jnp
from jax import lax
from jax.experimental import pallas as pl
from jax.experimental.pallas import tpu as pltpu
from jax.sharding import PartitionSpec as P

MESH = pl.DeviceIdType.MESH
F32 = jnp.float32
BF16 = jnp.bfloat16
LEV = 48
LANES = 128
PASSES = 4
NEAR = 2
CHUNK = 16
CHUNK_END = 48


def two_terms(x):
    high = x.astype(BF16)
    return high, (x - high.astype(F32)).astype(BF16)


def mul(a, b):
    return jnp.dot(a, b, preferred_element_type=F32)


def mul_terms(a, b):
    a_high, a_low = two_terms(a)
    b_high, b_low = two_terms(b)
    return mul(a_high, b_high) + mul(a_high, b_low) + mul(a_low, b_high)


def lane_of(shape):
    return lax.broadcasted_iota(jnp.int32, shape, len(shape) - 1)


def kernel(
    nz,
    ng,
    count,
    vals_hbm,
    weight_hbm,
    box_hbm,
    owner_hbm,
    dx_hbm,
    dy_hbm,
    sp_hbm,
    land_hbm,
    corr_hbm,
    out_v,
    weight,
    box,
    owner,
    land,
    corr,
    vals,
    raw,
    ext,
    edge,
    pack_s,
    pack_r,
    slab_s,
    slab_r,
    sums_s,
    sums_r,
    by_level,
    part_s,
    part_r,
    tile_s,
    tile_r,
    box_s,
    box_r,
    field,
    face_below,
    ready,
    local_sem,
    bulk_send,
    bulk_recv,
    pack_send,
    pack_recv,
    slab_send,
    slab_recv,
    all_send,
    all_recv,
    box_send,
    box_recv,
):
    group = 2 * ng
    per = LEV // ng
    rows1 = per * 8
    late = per // 3
    early = per - late
    late8 = late * 8
    rows3 = tile_r.shape[1]
    sent3 = -(-per // 4) * 4
    owners = nz * ng
    depth = group * 8
    gx = lax.axis_index("gx")
    gy = lax.axis_index("gy")
    half = lax.div(gx, nz)
    z = lax.rem(gx, nz)
    me = half * ng + gy

    nx = ng // 4
    y = 2 * lax.div(gy, ng // 2) + half
    x_core = lax.rem(gy, ng // 2)
    chip_x, core = lax.div(x_core, 2), lax.rem(x_core, 2)

    def hops(step, size):
        return min(step, size - step)

    offsets = sorted(
        (
            (oy, ox, oc)
            for oy in range(4)
            for ox in range(nx)
            for oc in range(2)
            if oy or ox or oc
        ),
        key=lambda o: (-hops(o[0], 4) - hops(o[1], nx), o[2], (o[0] + o[1]) % 4, o),
    )
    z_steps = sorted(range(1, nz), key=lambda step: (-hops(step, nz), step))

    def member(offset):
        to_y = lax.rem(y + offset[0], 4)
        to_x = lax.rem(chip_x + offset[1], nx)
        to_core = lax.rem(core + offset[2], 2)
        h = lax.rem(to_y, 2)
        g = lax.div(to_y, 2) * (ng // 2) + 2 * to_x + to_core
        return h * ng + g, (h * nz + z, g)

    def along_z(step):
        target = lax.rem(z + step, nz)
        return target, (half * nz + target, gy)

    east = (lax.rem(gx + 1, 2 * nz), gy)
    west = (lax.rem(gx + 2 * nz - 1, 2 * nz), gy)
    north = (gx, lax.rem(gy + 1, ng))
    south = (gx, lax.rem(gy + ng - 1, ng))

    def remote(src, dst, send, recv, device):
        return pltpu.make_async_remote_copy(
            src_ref=src,
            dst_ref=dst,
            send_sem=send,
            recv_sem=recv,
            device_id=device,
            device_id_type=MESH,
        )

    tile_r[...] = jnp.zeros(tile_r.shape, F32)
    tile_s[...] = jnp.zeros(tile_s.shape, F32)
    loads = [
        pltpu.make_async_copy(owner_hbm, owner, local_sem.at[0]),
        pltpu.make_async_copy(weight_hbm, weight, local_sem.at[1]),
        pltpu.make_async_copy(box_hbm, box, local_sem.at[2]),
        pltpu.make_async_copy(vals_hbm, vals, local_sem.at[3]),
        pltpu.make_async_copy(land_hbm, land, local_sem.at[4]),
        pltpu.make_async_copy(dx_hbm, raw.at[0], local_sem.at[5]),
        pltpu.make_async_copy(dy_hbm, raw.at[1], local_sem.at[6]),
        pltpu.make_async_copy(sp_hbm, raw.at[2], local_sem.at[7]),
        pltpu.make_async_copy(corr_hbm, corr, local_sem.at[8]),
    ]
    for load in loads[:4]:
        load.start()

    barrier = pltpu.get_barrier_semaphore()

    for device in (
        *(member(offset)[1] for offset in offsets),
        *(along_z(step)[1] for step in z_steps),
        east,
        west,
    ):
        pl.semaphore_signal(barrier, inc=1, device_id=device, device_id_type=MESH)
    for load in loads[4:]:
        load.start()

    for load in loads[:4]:
        load.wait()
    weighted = jnp.where(
        lax.broadcasted_iota(jnp.int32, (16, LANES), 0) < count[0], weight[...], 0.0
    )
    boxes = box[...]
    place = (boxes >> 6) * LANES + (boxes & 63)
    target = lax.broadcasted_iota(jnp.int32, (2 * LANES, LANES), 0)
    for j in range(8):
        terms = []
        hots = []
        for parity in range(2):
            b = 2 * j + parity
            value = vals[b].astype(F32) * weighted[b : b + 1, :]
            terms.append(two_terms(value))
            hit = target == place[b : b + 1, :] + 64 * parity
            hots.append(jnp.where(hit, 1.0, 0.0).astype(BF16))
        left = jnp.concatenate(
            [
                jnp.concatenate([terms[0][0], terms[1][0]], axis=1),
                jnp.concatenate([terms[0][1], terms[1][1]], axis=1),
            ],
            axis=0,
        )
        hot = jnp.concatenate(hots, axis=1)
        total = lax.dot_general(left, hot, (((1,), (1,)), ((), ())), preferred_element_type=F32)
        total = total[:LEV] + total[LEV:]
        by_level[0, pl.ds(j, LEV, stride=8), :] = total[:, :LANES]
        by_level[1, pl.ds(j, LEV, stride=8), :] = total[:, LANES:]

    lane1 = lane_of((1, LANES))
    base = lax.rem(me * 8, LANES)
    base_odd = lax.rem(me * 8 + 64, LANES)
    owner_row = jnp.zeros((1, LANES), F32)
    for j in range(8):
        owner_row = jnp.where(lane1 == base + j, owner[2 * j].astype(F32), owner_row)
        owner_row = jnp.where(lane1 == base_odd + j, owner[2 * j + 1].astype(F32), owner_row)
    for h in range(2):
        for g in range(ng):
            low = g * rows1
            sums_s[h * ng + g, late8:rows1, :] = by_level[h, low : low + rows1 - late8, :]
            sums_s[h * ng + g, 0:late8, :] = by_level[h, low + rows1 - late8 : low + rows1, :]
            sums_s[h * ng + g, rows1 : rows1 + 1, :] = owner_row

    for load in loads[4:]:
        load.wait()
    mask = land[...].astype(F32)
    for x in range(8):
        for a in range(3):
            value = raw[a, pl.ds(x, LEV, stride=8), :]
            if a == 2:
                value = value * mask[x : x + 1, :]
            ext[4 + x, a] = value

    lane = lane_of((LEV, LANES))
    for part in range(2):
        to_south = jnp.zeros((LEV, LANES), F32)
        to_north = jnp.zeros((LEV, LANES), F32)
        for r in range(4):
            for a in range(3):
                q = 3 * r + a
                value = ext[4 + 4 * part + r, a]
                if q:
                    value = pltpu.roll(value, 8 * q, 1)
                low = (8 * q + LANES - 4) % LANES
                to_south = jnp.where((lane >= 8 * q) & (lane < 8 * q + 4), value, to_south)
                to_north = jnp.where((lane >= low) & (lane < low + 4), value, to_north)
        pack_s[0, part] = to_south
        pack_s[1, part] = to_north
    packs = [
        remote(pack_s.at[0], pack_r.at[0], pack_send.at[0], pack_recv.at[0], south),
        remote(pack_s.at[1], pack_r.at[1], pack_send.at[1], pack_recv.at[1], north),
    ]
    pl.semaphore_wait(barrier, group + nz)
    for copy in packs:
        copy.start()


    early_rows = pl.ds(late8, rows1 + 1 - late8)
    late_rows = pl.ds(0, late8)
    for k, rows in enumerate((early_rows, late_rows)):
        for offset in offsets:
            index, device = member(offset)
            remote(
                sums_s.at[index, rows],
                sums_r.at[me, rows],
                all_send.at[k],
                all_recv.at[k],
                device,
            ).start()
    sums_r[me] = sums_s[me]

    for copy in packs:
        copy.wait()
    for part in range(2):
        from_north = jnp.where(gy < ng - 1, pack_r[0, part], 0.0)
        from_south = jnp.where(gy > 0, pack_r[1, part], 0.0)
        slab_s[part] = jnp.where((lane & 7) < 4, from_north, from_south)
    slabs = [
        remote(slab_s.at[0], slab_r.at[1], slab_send.at[0], slab_recv.at[0], west),
        remote(slab_s.at[1], slab_r.at[0], slab_send.at[1], slab_recv.at[1], east),
    ]
    for copy in slabs:
        copy.start()
    def rows_to_neighbours(index, low, size):
        return [
            remote(
                ext.at[pl.ds(4 + low, size)],
                ext.at[pl.ds(12 + low, size)],
                bulk_send.at[index, 0],
                bulk_recv.at[index, 0],
                west,
            ),
            remote(
                ext.at[pl.ds(12 - low - size, size)],
                ext.at[pl.ds(4 - low - size, size)],
                bulk_send.at[index, 1],
                bulk_recv.at[index, 1],
                east,
            ),
        ]

    bulk = rows_to_neighbours(0, 0, NEAR)
    for copy in bulk:
        copy.start()

    level = lax.broadcasted_iota(jnp.int32, (LEV, ng * rows3), 0)
    column = lane_of((LEV, ng * rows3))
    from_group = column // rows3
    within = column - from_group * rows3
    chosen = (within < per) & (from_group * per + within == level)
    corr_v = corr[...]
    corr_rows = jnp.dot(
        corr_v,
        jnp.where(chosen, 1.0, 0.0),
        precision=lax.Precision.HIGHEST,
        preferred_element_type=F32,
    )

    for copy in slabs:
        copy.wait()
    outer = (lane < 4) | (lane >= LANES - 4)
    for part in range(4):
        slab = (slab_r[0], slab_s[0], slab_s[1], slab_r[1])[part]
        for r in range(4):
            for a in range(3):
                q = 3 * r + a
                value = pltpu.roll(slab, LANES - 8 * q, 1) if q else slab
                edge[4 * part + r, a] = jnp.where(outer, value, 0.0)

    def wait_bytes(ref, sem, size):
        view = ref.at[pl.ds(0, size)]
        pltpu.make_async_copy(view, view, sem).wait()

    wait_bytes(sums_r.at[:, early_rows], all_recv.at[0], group - 1)
    wide = (depth + LANES - 1) // LANES
    owner_rows = []
    for parity in range(2):
        pieces = []
        for piece in range(wide):
            row = jnp.zeros((1, LANES), F32)
            for source in range(piece * 16, min(group, piece * 16 + 16)):
                start = (source * 8 + 64 * parity) % LANES
                row = jnp.where(
                    (lane1 >= start) & (lane1 < start + 8),
                    sums_r[source, rows1 : rows1 + 1, :],
                    row,
                )
            pieces.append(pltpu.roll(row, 64, 1) if parity else row)
        row = jnp.concatenate(pieces, axis=1) if wide > 1 else pieces[0]
        owner_rows.append(row[:, :depth])
    candidate = lax.broadcasted_iota(jnp.int32, (owners, depth), 0)
    even, odd = (row.astype(jnp.int32) for row in owner_rows)

    def hits(row, shift):
        return jnp.where(row == candidate + shift, 1.0, 0.0).astype(BF16)

    left = jnp.concatenate(
        [
            jnp.concatenate([hits(even, 0), hits(odd, 0)], axis=1),
            jnp.concatenate([hits(odd, owners), hits(even, owners)], axis=1),
        ],
        axis=0,
    )
    lower = lane_of((owners, LANES)) < 64

    def add_by_owner(k, first_level, levels, first_row):
        columns = []
        for t in range(levels):
            low = first_row + 8 * t
            value = sums_r[:, low : low + 8, :].reshape(depth, LANES)
            columns.append(jnp.concatenate([value, pltpu.roll(value, 64, 1)], axis=0))
        stack_high, stack_low = two_terms(jnp.concatenate(columns, axis=1))
        by_owner = mul(left, stack_high) + mul(left, stack_low)
        for t in range(levels):
            cut = by_owner[:, t * LANES : (t + 1) * LANES]
            part_s[:, first_level + t] = jnp.where(
                lower, cut[:owners], cut[owners:]
            ).reshape(nz, ng, LANES)
        for step in z_steps:
            index, device = along_z(step)
            chosen_levels = pl.ds(first_level, levels)
            remote(
                part_s.at[index, chosen_levels],
                part_r.at[z, chosen_levels],
                all_send.at[2 + k],
                all_recv.at[2 + k],
                device,
            ).start()

    add_by_owner(0, 0, early, late8)
    wait_bytes(sums_r.at[:, late_rows], all_recv.at[1], group - 1)
    add_by_owner(1, early, late, 0)
    part_r[z] = part_s[z]

    for copy in bulk:
        copy.wait()

    def faces(x, _):
        here, beyond = ext[x, 2], edge[x, 2]
        last = lane == LANES - 1
        turned, turned_beyond = pltpu.roll(here, LANES - 1, 1), pltpu.roll(beyond, LANES - 1, 1)
        ext[x, 0] = jnp.where(here * ext[x + 1, 2] > 0.0, ext[x, 0], 0.0)
        edge[x, 0] = jnp.where(beyond * edge[x + 1, 2] > 0.0, edge[x, 0], 0.0)
        upper = jnp.where(last, turned_beyond, turned)
        upper_beyond = jnp.where(last, turned, turned_beyond)
        north_face = jnp.where(here * upper > 0.0, ext[x, 1], 0.0)
        north_face_beyond = jnp.where(beyond * upper_beyond > 0.0, edge[x, 1], 0.0)
        turned, turned_beyond = pltpu.roll(north_face, 1, 1), pltpu.roll(north_face_beyond, 1, 1)
        ext[x, 1] = north_face
        edge[x, 1] = north_face_beyond
        face_below[x, 0] = jnp.where(lane == 0, turned_beyond, turned)
        face_below[x, 1] = jnp.where(lane == 0, turned, turned_beyond)
        return _

    lax.fori_loop(4 - NEAR, 11 + NEAR, faces, 0)

    parts = [
        (part_r.at[:, pl.ds(0, early)], 2),
        (part_r.at[:, pl.ds(early, late)], 3),
    ]
    wait_bytes(parts[0][0], all_recv.at[2], nz - 1)
    row = lax.broadcasted_iota(jnp.int32, (ng, LANES), 0)
    box_column = lane_of((ng, LANES)) & 15
    low_boxes = lane_of((ng, LANES)) < 64
    for t in range(per):
        if t == early:
            wait_bytes(parts[1][0], all_recv.at[3], nz - 1)
        value = part_r[0, t]
        for source in range(1, nz):
            value = value + part_r[source, t]
        below = jnp.where(row == 0, 0.0, pltpu.roll(value, 1, 0))
        above = jnp.where(row == ng - 1, 0.0, pltpu.roll(value, ng - 1, 0))
        near = jnp.where(box_column == 15, below, above)
        other, other_near = pltpu.roll(value, 64, 1), pltpu.roll(near, 64, 1)
        tile_s[pl.ds(t, ng, stride=rows3), :] = jnp.where(low_boxes, value, other_near)
        tile_s[pl.ds(ng * rows3 + t, ng, stride=rows3), :] = jnp.where(low_boxes, other, near)

    first_rows = pl.ds(0, sent3)
    for offset in offsets:
        index, device = member(offset)
        start = pl.multiple_of(index * rows3, 8)
        remote(
            tile_s.at[pl.ds(start, sent3)],
            tile_r.at[me, first_rows],
            all_send.at[4],
            all_recv.at[4],
            device,
        ).start()
    far = rows_to_neighbours(1, NEAR, 4 - NEAR)
    for copy in far:
        copy.start()
    tile_r[me] = tile_s[pl.ds(pl.multiple_of(me * rows3, 8), rows3), :]

    wait_bytes(tile_r.at[:, first_rows], all_recv.at[4], group - 1)
    arrived = jnp.concatenate(
        [tile_r[h * ng : (h + 1) * ng].reshape(ng * rows3, LANES) for h in range(2)], axis=1
    )
    mixed = mul_terms(corr_rows, arrived)
    for h in range(2):
        box_s[h] = mixed[:, h * LANES : (h + 1) * LANES]
    borders = [
        remote(box_s.at[0], box_r.at[1], box_send.at[0], box_recv.at[0], west),
        remote(box_s.at[1], box_r.at[0], box_send.at[1], box_recv.at[1], east),
    ]
    for copy in borders:
        copy.start()

    def levels_of(step, size):
        rows = pl.ds(pl.multiple_of(step * size, 8), size)
        lanes = lane_of((size, LANES))
        first, last = lanes == 0, lanes == LANES - 1

        def forced(part, source):
            value = source[rows, :]
            made = {}
            for r in range(4):
                x = 4 * part + r
                at_inner = 16 * r + (lanes >> 3)
                at_outside = jnp.where(lanes < 64, 64 + 16 * r, 64 + 16 * r + 15)
                made[x] = (
                    ext[x, 2, rows, :] * jnp.take_along_axis(value, at_inner, axis=1),
                    edge[x, 2, rows, :] * jnp.take_along_axis(value, at_outside, axis=1),
                )
            return made

        def passed(turn, chosen, state):
            needed = sorted({x - 1 for x in chosen} | set(chosen))
            turned = {
                x: [pltpu.roll(state[x][k], shift, 1) for shift in (LANES - 1, 1) for k in range(2)]
                for x in chosen
            }
            result = {x: [None, None] for x in chosen}
            for k, faces_of in enumerate((ext, edge)):
                if k and turn == PASSES - 1:
                    break
                flow = {
                    x: faces_of[x, 0, rows, :] * (state[x + 1][k] - state[x][k]) for x in needed
                }
                for x in chosen:
                    here = state[x][k]
                    above, below = turned[x][:2], turned[x][2:]
                    up = faces_of[x, 1, rows, :] * (
                        jnp.where(last, above[1 - k], above[k]) - here
                    )
                    down = face_below[x, k, rows, :] * (
                        jnp.where(first, below[1 - k], below[k]) - here
                    )
                    result[x][k] = here + (flow[x] - flow[x - 1]) + (up + down)
            return result

        return rows, forced, passed

    def begin(step, _):
        rows, forced, passed = levels_of(step, CHUNK)
        state = {**forced(1, box_s.at[0]), **forced(2, box_s.at[1])}
        for turn in range(PASSES):
            for x in state:
                for k in range(2):
                    ready[turn, x - 4, k, rows, :] = state[x][k]
            if turn < PASSES - 1:
                state = passed(turn, range(5 + turn, 11 - turn), state)
        return _

    def finish(step, _):
        rows, forced, passed = levels_of(step, CHUNK_END)

        def known(turn):
            return {
                x: [ready[turn, x - 4, k, rows, :] for k in range(2)]
                for x in range(4 + turn, 12 - turn)
            }

        state = {**forced(0, box_r.at[0]), **known(0), **forced(3, box_r.at[1])}
        for turn in range(PASSES):
            chosen = [
                x
                for x in range(1 + turn, 15 - turn)
                if turn == PASSES - 1 or not 5 + turn <= x < 11 - turn
            ]
            new = passed(turn, chosen, state)
            state = new if turn == PASSES - 1 else {**new, **known(turn + 1)}
        for x in range(8):
            field[x, rows, :] = state[4 + x][0]
        return _

    lax.fori_loop(0, LEV // CHUNK, begin, 0)
    for copy in far:
        copy.wait()
    lax.fori_loop(0, 4 - NEAR, faces, 0)
    lax.fori_loop(11 + NEAR, 15, faces, 0)
    for copy in borders:
        copy.wait()
    lax.fori_loop(0, LEV // CHUNK_END, finish, 0)

    whole = jnp.concatenate([field[x] for x in range(8)], axis=1)
    result = mul_terms(corr_v, whole)
    for x in range(8):
        out_v[pl.ds(x, LEV, stride=8), :] = ext[4 + x, 2] * result[:, x * LANES : (x + 1) * LANES]

    wait_bytes(sums_r.at[:, early_rows], all_send.at[0], group - 1)
    wait_bytes(sums_r.at[:, late_rows], all_send.at[1], group - 1)
    for ref, k in parts:
        wait_bytes(ref, all_send.at[k], nz - 1)
    wait_bytes(tile_r.at[:, first_rows], all_send.at[4], group - 1)


def local(
    nz,
    ng,
    obs_values,
    obs_weight,
    obs_box,
    obs_owner,
    block_count,
    diff_x,
    diff_y,
    spread_std,
    land_sea,
    vert_corr,
):
    group = 2 * ng
    per = LEV // ng
    rows3 = -(-per // 8) * 8
    hbm = pl.BlockSpec(memory_space=pltpu.HBM)
    dma = pltpu.SemaphoreType.DMA
    flat = (LEV * 8, LANES)
    out = pl.pallas_call(
        functools.partial(kernel, nz, ng),
        out_shape=jax.ShapeDtypeStruct(flat, F32),
        in_specs=[pl.BlockSpec(memory_space=pltpu.SMEM)] + [hbm] * 9,
        out_specs=pl.BlockSpec(memory_space=pltpu.VMEM),
        scratch_shapes=[
            pltpu.VMEM((16, LANES), F32),
            pltpu.VMEM((16, LANES), jnp.int32),
            pltpu.SMEM((16,), jnp.int32),
            pltpu.VMEM((8, LANES), jnp.int32),
            pltpu.VMEM((LEV, LEV), F32),
            pltpu.VMEM((16, LEV, LANES), BF16),
            pltpu.VMEM((3,) + flat, F32),
            pltpu.VMEM((16, 3, LEV, LANES), F32),
            pltpu.VMEM((16, 3, LEV, LANES), F32),
            pltpu.VMEM((2, 2, LEV, LANES), F32),
            pltpu.VMEM((2, 2, LEV, LANES), F32),
            pltpu.VMEM((2, LEV, LANES), F32),
            pltpu.VMEM((2, LEV, LANES), F32),
            pltpu.VMEM((group, per * 8 + 1, LANES), F32),
            pltpu.VMEM((group, per * 8 + 1, LANES), F32),
            pltpu.VMEM((2,) + flat, F32),
            pltpu.VMEM((nz, per, ng, LANES), F32),
            pltpu.VMEM((nz, per, ng, LANES), F32),
            pltpu.VMEM((group * rows3, LANES), F32),
            pltpu.VMEM((group, rows3, LANES), F32),
            pltpu.VMEM((2, LEV, LANES), F32),
            pltpu.VMEM((2, LEV, LANES), F32),
            pltpu.VMEM((8, LEV, LANES), F32),
            pltpu.VMEM((16, 2, LEV, LANES), F32),
            pltpu.VMEM((PASSES, 8, 2, LEV, LANES), F32),
            dma((9,)),
            dma((2, 2)),
            dma((2, 2)),
            dma((2,)),
            dma((2,)),
            dma((2,)),
            dma((2,)),
            dma((5,)),
            dma((5,)),
            dma((2,)),
            dma((2,)),
        ],
        compiler_params=pltpu.CompilerParams(
            collective_id=0, has_side_effects=True, vmem_limit_bytes=40 * 1024 * 1024
        ),
        name="analysis",
    )(
        block_count,
        *(
            pltpu.with_memory_space_constraint(value, pltpu.HBM)
            for value in (
                obs_values,
                obs_weight,
                obs_box,
                obs_owner,
                diff_x.reshape(flat),
                diff_y.reshape(flat),
                spread_std.reshape(flat),
                land_sea,
                vert_corr,
            )
        ),
    )
    return out.reshape(LEV, 8, LANES)


def solution(mesh):
    in_specs = (
        P(("gx", "gy"), None, None),
        P(("gx", "gy"), None),
        P(("gx", "gy"), None),
        P(("gx", "gy")),
        P(("gx", "gy")),
        P(None, "gx", "gy"),
        P(None, "gx", "gy"),
        P(None, "gx", "gy"),
        P("gx", "gy"),
        P(),
    )
    return jax.shard_map(
        functools.partial(local, mesh.shape["gx"] // 2, mesh.shape["gy"]),
        mesh=mesh,
        in_specs=in_specs,
        out_specs=P(None, "gx", "gy"),
        check_vma=False,
    )
```

```python
import functools

import jax
import jax.numpy as jnp
from jax import lax
from jax.experimental import pallas as pl
from jax.experimental.pallas import tpu as pltpu
from jax.sharding import PartitionSpec as P

MESH = pl.DeviceIdType.MESH
F32 = jnp.float32
BF16 = jnp.bfloat16
LEV = 48
LANES = 128
PASSES = 4
NEAR = 2
CHUNK = 16
CHUNK_END = 48


def two_terms(x):
    high = x.astype(BF16)
    return high, (x - high.astype(F32)).astype(BF16)


def mul(a, b):
    return jnp.dot(a, b, preferred_element_type=F32)


def mul_terms(a, b):
    a_high, a_low = two_terms(a)
    b_high, b_low = two_terms(b)
    return mul(a_high, b_high) + mul(a_high, b_low) + mul(a_low, b_high)


def lane_of(shape):
    return lax.broadcasted_iota(jnp.int32, shape, len(shape) - 1)


def kernel(
    nz,
    ng,
    count,
    vals_hbm,
    weight_hbm,
    box_hbm,
    owner_hbm,
    dx_hbm,
    dy_hbm,
    sp_hbm,
    land_hbm,
    corr_hbm,
    out_v,
    weight,
    box,
    owner,
    land,
    corr,
    vals,
    raw,
    ext,
    edge,
    pack_s,
    pack_r,
    slab_s,
    slab_r,
    sums_s,
    sums_r,
    by_level,
    part_s,
    part_r,
    tile_s,
    tile_r,
    box_s,
    box_r,
    field,
    face_below,
    ready,
    local_sem,
    bulk_send,
    bulk_recv,
    edge_send,
    edge_recv,
    pack_send,
    pack_recv,
    slab_send,
    slab_recv,
    all_send,
    all_recv,
    box_send,
    box_recv,
):
    group = 2 * ng
    per = LEV // ng
    rows1 = per * 8
    late = per // 3
    early = per - late
    late8 = late * 8
    rows3 = tile_r.shape[1]
    sent3 = -(-per // 4) * 4
    owners = nz * ng
    depth = group * 8
    gx = lax.axis_index("gx")
    gy = lax.axis_index("gy")
    half = lax.div(gx, nz)
    z = lax.rem(gx, nz)
    me = half * ng + gy

    nx = ng // 4
    y = 2 * lax.div(gy, ng // 2) + half
    x_core = lax.rem(gy, ng // 2)
    chip_x, core = lax.div(x_core, 2), lax.rem(x_core, 2)

    def hops(step, size):
        return min(step, size - step)

    offsets = sorted(
        (
            (oy, ox, oc)
            for oy in range(4)
            for ox in range(nx)
            for oc in range(2)
            if oy or ox or oc
        ),
        key=lambda o: (-hops(o[0], 4) - hops(o[1], nx), o[2], (o[0] + o[1]) % 4, o),
    )
    z_steps = sorted(range(1, nz), key=lambda step: (-hops(step, nz), step))

    def member(offset):
        to_y = lax.rem(y + offset[0], 4)
        to_x = lax.rem(chip_x + offset[1], nx)
        to_core = lax.rem(core + offset[2], 2)
        h = lax.rem(to_y, 2)
        g = lax.div(to_y, 2) * (ng // 2) + 2 * to_x + to_core
        return h * ng + g, (h * nz + z, g)

    def along_z(step):
        target = lax.rem(z + step, nz)
        return target, (half * nz + target, gy)

    east = (lax.rem(gx + 1, 2 * nz), gy)
    west = (lax.rem(gx + 2 * nz - 1, 2 * nz), gy)
    north = (gx, lax.rem(gy + 1, ng))
    south = (gx, lax.rem(gy + ng - 1, ng))

    def remote(src, dst, send, recv, device):
        return pltpu.make_async_remote_copy(
            src_ref=src,
            dst_ref=dst,
            send_sem=send,
            recv_sem=recv,
            device_id=device,
            device_id_type=MESH,
        )

    tile_r[...] = jnp.zeros(tile_r.shape, F32)
    tile_s[...] = jnp.zeros(tile_s.shape, F32)
    loads = [
        pltpu.make_async_copy(owner_hbm, owner, local_sem.at[0]),
        pltpu.make_async_copy(weight_hbm, weight, local_sem.at[1]),
        pltpu.make_async_copy(box_hbm, box, local_sem.at[2]),
        pltpu.make_async_copy(vals_hbm, vals, local_sem.at[3]),
        pltpu.make_async_copy(land_hbm, land, local_sem.at[4]),
        pltpu.make_async_copy(dx_hbm, raw.at[0], local_sem.at[5]),
        pltpu.make_async_copy(dy_hbm, raw.at[1], local_sem.at[6]),
        pltpu.make_async_copy(sp_hbm, raw.at[2], local_sem.at[7]),
        pltpu.make_async_copy(corr_hbm, corr, local_sem.at[8]),
    ]
    for load in loads[:4]:
        load.start()

    barrier = pltpu.get_barrier_semaphore()

    for device in (
        *(member(offset)[1] for offset in offsets),
        *(along_z(step)[1] for step in z_steps),
        east,
        west,
    ):
        pl.semaphore_signal(barrier, inc=1, device_id=device, device_id_type=MESH)
    for load in loads[4:]:
        load.start()

    for load in loads[:4]:
        load.wait()
    weighted = jnp.where(
        lax.broadcasted_iota(jnp.int32, (16, LANES), 0) < count[0], weight[...], 0.0
    )
    boxes = box[...]
    place = (boxes >> 6) * LANES + (boxes & 63)
    target = lax.broadcasted_iota(jnp.int32, (2 * LANES, LANES), 0)
    for j in range(8):
        terms = []
        hots = []
        for parity in range(2):
            b = 2 * j + parity
            value = vals[b].astype(F32) * weighted[b : b + 1, :]
            terms.append(two_terms(value))
            hit = target == place[b : b + 1, :] + 64 * parity
            hots.append(jnp.where(hit, 1.0, 0.0).astype(BF16))
        left = jnp.concatenate(
            [
                jnp.concatenate([terms[0][0], terms[1][0]], axis=1),
                jnp.concatenate([terms[0][1], terms[1][1]], axis=1),
            ],
            axis=0,
        )
        hot = jnp.concatenate(hots, axis=1)
        total = lax.dot_general(left, hot, (((1,), (1,)), ((), ())), preferred_element_type=F32)
        total = total[:LEV] + total[LEV:]
        by_level[0, pl.ds(j, LEV, stride=8), :] = total[:, :LANES]
        by_level[1, pl.ds(j, LEV, stride=8), :] = total[:, LANES:]

    lane1 = lane_of((1, LANES))
    base = lax.rem(me * 8, LANES)
    base_odd = lax.rem(me * 8 + 64, LANES)
    owner_row = jnp.zeros((1, LANES), F32)
    for j in range(8):
        owner_row = jnp.where(lane1 == base + j, owner[2 * j].astype(F32), owner_row)
        owner_row = jnp.where(lane1 == base_odd + j, owner[2 * j + 1].astype(F32), owner_row)
    for h in range(2):
        for g in range(ng):
            low = g * rows1
            sums_s[h * ng + g, late8:rows1, :] = by_level[h, low : low + rows1 - late8, :]
            sums_s[h * ng + g, 0:late8, :] = by_level[h, low + rows1 - late8 : low + rows1, :]
            sums_s[h * ng + g, rows1 : rows1 + 1, :] = owner_row

    for load in loads[4:]:
        load.wait()
    mask = land[...].astype(F32)
    for x in range(8):
        for a in range(3):
            value = raw[a, pl.ds(x, LEV, stride=8), :]
            if a == 2:
                value = value * mask[x : x + 1, :]
            ext[4 + x, a] = value

    lane = lane_of((LEV, LANES))
    for part in range(2):
        to_south = jnp.zeros((LEV, LANES), F32)
        to_north = jnp.zeros((LEV, LANES), F32)
        for r in range(4):
            for a in range(3):
                q = 3 * r + a
                value = ext[4 + 4 * part + r, a]
                if q:
                    value = pltpu.roll(value, 8 * q, 1)
                low = (8 * q + LANES - 4) % LANES
                to_south = jnp.where((lane >= 8 * q) & (lane < 8 * q + 4), value, to_south)
                to_north = jnp.where((lane >= low) & (lane < low + 4), value, to_north)
        pack_s[0, part] = to_south
        pack_s[1, part] = to_north
    packs = [
        remote(pack_s.at[0], pack_r.at[0], pack_send.at[0], pack_recv.at[0], south),
        remote(pack_s.at[1], pack_r.at[1], pack_send.at[1], pack_recv.at[1], north),
    ]
    pl.semaphore_wait(barrier, group + nz)
    for copy in packs:
        copy.start()


    early_rows = pl.ds(late8, rows1 + 1 - late8)
    late_rows = pl.ds(0, late8)
    for k, rows in enumerate((early_rows, late_rows)):
        for offset in offsets:
            index, device = member(offset)
            remote(
                sums_s.at[index, rows],
                sums_r.at[me, rows],
                all_send.at[k],
                all_recv.at[k],
                device,
            ).start()
    sums_r[me] = sums_s[me]

    for copy in packs:
        copy.wait()
    for part in range(2):
        from_north = jnp.where(gy < ng - 1, pack_r[0, part], 0.0)
        from_south = jnp.where(gy > 0, pack_r[1, part], 0.0)
        slab_s[part] = jnp.where((lane & 7) < 4, from_north, from_south)
    slabs = [
        remote(slab_s.at[0], slab_r.at[1], slab_send.at[0], slab_recv.at[0], west),
        remote(slab_s.at[1], slab_r.at[0], slab_send.at[1], slab_recv.at[1], east),
    ]
    for copy in slabs:
        copy.start()
    def rows_to_neighbours(index, low, size):
        return [
            remote(
                ext.at[pl.ds(4 + low, size)],
                ext.at[pl.ds(12 + low, size)],
                bulk_send.at[index, 0],
                bulk_recv.at[index, 0],
                west,
            ),
            remote(
                ext.at[pl.ds(12 - low - size, size)],
                ext.at[pl.ds(4 - low - size, size)],
                bulk_send.at[index, 1],
                bulk_recv.at[index, 1],
                east,
            ),
        ]

    bulk = rows_to_neighbours(0, 0, NEAR)
    for copy in bulk:
        copy.start()

    level = lax.broadcasted_iota(jnp.int32, (LEV, ng * rows3), 0)
    column = lane_of((LEV, ng * rows3))
    from_group = column // rows3
    within = column - from_group * rows3
    chosen = (within < per) & (from_group * per + within == level)
    corr_v = corr[...]
    corr_rows = jnp.dot(
        corr_v,
        jnp.where(chosen, 1.0, 0.0),
        precision=lax.Precision.HIGHEST,
        preferred_element_type=F32,
    )

    for copy in slabs:
        copy.wait()
    outer = (lane < 4) | (lane >= LANES - 4)
    for part in range(4):
        slab = (slab_r[0], slab_s[0], slab_s[1], slab_r[1])[part]
        for r in range(4):
            for a in range(3):
                q = 3 * r + a
                value = pltpu.roll(slab, LANES - 8 * q, 1) if q else slab
                edge[4 * part + r, a] = jnp.where(outer, value, 0.0)

    def wait_bytes(ref, sem, size):
        view = ref.at[pl.ds(0, size)]
        pltpu.make_async_copy(view, view, sem).wait()

    wait_bytes(sums_r.at[:, early_rows], all_recv.at[0], group - 1)
    wide = (depth + LANES - 1) // LANES
    owner_rows = []
    for parity in range(2):
        pieces = []
        for piece in range(wide):
            row = jnp.zeros((1, LANES), F32)
            for source in range(piece * 16, min(group, piece * 16 + 16)):
                start = (source * 8 + 64 * parity) % LANES
                row = jnp.where(
                    (lane1 >= start) & (lane1 < start + 8),
                    sums_r[source, rows1 : rows1 + 1, :],
                    row,
                )
            pieces.append(pltpu.roll(row, 64, 1) if parity else row)
        row = jnp.concatenate(pieces, axis=1) if wide > 1 else pieces[0]
        owner_rows.append(row[:, :depth])
    candidate = lax.broadcasted_iota(jnp.int32, (owners, depth), 0)
    even, odd = (row.astype(jnp.int32) for row in owner_rows)

    def hits(row, shift):
        return jnp.where(row == candidate + shift, 1.0, 0.0).astype(BF16)

    left = jnp.concatenate(
        [
            jnp.concatenate([hits(even, 0), hits(odd, 0)], axis=1),
            jnp.concatenate([hits(odd, owners), hits(even, owners)], axis=1),
        ],
        axis=0,
    )
    lower = lane_of((owners, LANES)) < 64

    def add_by_owner(k, first_level, levels, first_row):
        columns = []
        for t in range(levels):
            low = first_row + 8 * t
            value = sums_r[:, low : low + 8, :].reshape(depth, LANES)
            columns.append(jnp.concatenate([value, pltpu.roll(value, 64, 1)], axis=0))
        stack_high, stack_low = two_terms(jnp.concatenate(columns, axis=1))
        by_owner = mul(left, stack_high) + mul(left, stack_low)
        for t in range(levels):
            cut = by_owner[:, t * LANES : (t + 1) * LANES]
            part_s[:, first_level + t] = jnp.where(
                lower, cut[:owners], cut[owners:]
            ).reshape(nz, ng, LANES)
        for step in z_steps:
            index, device = along_z(step)
            chosen_levels = pl.ds(first_level, levels)
            remote(
                part_s.at[index, chosen_levels],
                part_r.at[z, chosen_levels],
                all_send.at[2 + k],
                all_recv.at[2 + k],
                device,
            ).start()

    add_by_owner(0, 0, early, late8)
    wait_bytes(sums_r.at[:, late_rows], all_recv.at[1], group - 1)
    add_by_owner(1, early, late, 0)
    part_r[z] = part_s[z]

    for copy in bulk:
        copy.wait()

    def faces(x, _):
        here, beyond = ext[x, 2], edge[x, 2]
        last = lane == LANES - 1
        turned, turned_beyond = pltpu.roll(here, LANES - 1, 1), pltpu.roll(beyond, LANES - 1, 1)
        ext[x, 0] = jnp.where(here * ext[x + 1, 2] > 0.0, ext[x, 0], 0.0)
        edge[x, 0] = jnp.where(beyond * edge[x + 1, 2] > 0.0, edge[x, 0], 0.0)
        upper = jnp.where(last, turned_beyond, turned)
        upper_beyond = jnp.where(last, turned, turned_beyond)
        north_face = jnp.where(here * upper > 0.0, ext[x, 1], 0.0)
        north_face_beyond = jnp.where(beyond * upper_beyond > 0.0, edge[x, 1], 0.0)
        turned, turned_beyond = pltpu.roll(north_face, 1, 1), pltpu.roll(north_face_beyond, 1, 1)
        ext[x, 1] = north_face
        edge[x, 1] = north_face_beyond
        face_below[x, 0] = jnp.where(lane == 0, turned_beyond, turned)
        face_below[x, 1] = jnp.where(lane == 0, turned, turned_beyond)
        return _

    lax.fori_loop(4 - NEAR, 11 + NEAR, faces, 0)

    parts = [
        (part_r.at[:, pl.ds(0, early)], 2),
        (part_r.at[:, pl.ds(early, late)], 3),
    ]
    wait_bytes(parts[0][0], all_recv.at[2], nz - 1)
    row = lax.broadcasted_iota(jnp.int32, (ng, LANES), 0)
    box_column = lane_of((ng, LANES)) & 15
    low_boxes = lane_of((ng, LANES)) < 64
    for t in range(per):
        if t == early:
            wait_bytes(parts[1][0], all_recv.at[3], nz - 1)
        value = part_r[0, t]
        for source in range(1, nz):
            value = value + part_r[source, t]
        below = jnp.where(row == 0, 0.0, pltpu.roll(value, 1, 0))
        above = jnp.where(row == ng - 1, 0.0, pltpu.roll(value, ng - 1, 0))
        near = jnp.where(box_column == 15, below, above)
        other, other_near = pltpu.roll(value, 64, 1), pltpu.roll(near, 64, 1)
        tile_s[pl.ds(t, ng, stride=rows3), :] = jnp.where(low_boxes, value, other_near)
        tile_s[pl.ds(ng * rows3 + t, ng, stride=rows3), :] = jnp.where(low_boxes, other, near)

    first_rows = pl.ds(0, sent3)
    for offset in offsets:
        index, device = member(offset)
        start = pl.multiple_of(index * rows3, 8)
        remote(
            tile_s.at[pl.ds(start, sent3)],
            tile_r.at[me, first_rows],
            all_send.at[4],
            all_recv.at[4],
            device,
        ).start()
    far = rows_to_neighbours(1, NEAR, 3 - NEAR)
    for k, (source, target, device) in enumerate(
        (
            (ext.at[7, 2], ext.at[15, 2], west),
            (ext.at[8, 0], ext.at[0, 0], east),
            (ext.at[8, 2], ext.at[0, 2], east),
        )
    ):
        far.append(remote(source, target, edge_send.at[k], edge_recv.at[k], device))
    for copy in far:
        copy.start()
    tile_r[me] = tile_s[pl.ds(pl.multiple_of(me * rows3, 8), rows3), :]

    wait_bytes(tile_r.at[:, first_rows], all_recv.at[4], group - 1)
    arrived = jnp.concatenate(
        [tile_r[h * ng : (h + 1) * ng].reshape(ng * rows3, LANES) for h in range(2)], axis=1
    )
    mixed = mul_terms(corr_rows, arrived)
    for h in range(2):
        box_s[h] = mixed[:, h * LANES : (h + 1) * LANES]
    borders = [
        remote(box_s.at[0], box_r.at[1], box_send.at[0], box_recv.at[0], west),
        remote(box_s.at[1], box_r.at[0], box_send.at[1], box_recv.at[1], east),
    ]
    for copy in borders:
        copy.start()

    def levels_of(step, size):
        rows = pl.ds(pl.multiple_of(step * size, 8), size)
        lanes = lane_of((size, LANES))
        first, last = lanes == 0, lanes == LANES - 1

        def forced(part, source):
            value = source[rows, :]
            made = {}
            for r in range(4):
                x = 4 * part + r
                at_inner = 16 * r + (lanes >> 3)
                at_outside = jnp.where(lanes < 64, 64 + 16 * r, 64 + 16 * r + 15)
                made[x] = (
                    ext[x, 2, rows, :] * jnp.take_along_axis(value, at_inner, axis=1),
                    edge[x, 2, rows, :] * jnp.take_along_axis(value, at_outside, axis=1),
                )
            return made

        def passed(turn, chosen, state):
            needed = sorted({x - 1 for x in chosen} | set(chosen))
            turned = {
                x: [pltpu.roll(state[x][k], shift, 1) for shift in (LANES - 1, 1) for k in range(2)]
                for x in chosen
            }
            result = {x: [None, None] for x in chosen}
            for k, faces_of in enumerate((ext, edge)):
                if k and turn == PASSES - 1:
                    break
                flow = {
                    x: faces_of[x, 0, rows, :] * (state[x + 1][k] - state[x][k]) for x in needed
                }
                for x in chosen:
                    here = state[x][k]
                    above, below = turned[x][:2], turned[x][2:]
                    up = faces_of[x, 1, rows, :] * (
                        jnp.where(last, above[1 - k], above[k]) - here
                    )
                    down = face_below[x, k, rows, :] * (
                        jnp.where(first, below[1 - k], below[k]) - here
                    )
                    result[x][k] = here + (flow[x] - flow[x - 1]) + (up + down)
            return result

        return rows, forced, passed

    def begin(step, _):
        rows, forced, passed = levels_of(step, CHUNK)
        state = {**forced(1, box_s.at[0]), **forced(2, box_s.at[1])}
        for turn in range(PASSES):
            for x in state:
                for k in range(2):
                    ready[turn, x - 4, k, rows, :] = state[x][k]
            if turn < PASSES - 1:
                state = passed(turn, range(5 + turn, 11 - turn), state)
        return _

    def finish(step, _):
        rows, forced, passed = levels_of(step, CHUNK_END)

        def known(turn):
            return {
                x: [ready[turn, x - 4, k, rows, :] for k in range(2)]
                for x in range(4 + turn, 12 - turn)
            }

        state = {**forced(0, box_r.at[0]), **known(0), **forced(3, box_r.at[1])}
        for turn in range(PASSES):
            chosen = [
                x
                for x in range(1 + turn, 15 - turn)
                if turn == PASSES - 1 or not 5 + turn <= x < 11 - turn
            ]
            new = passed(turn, chosen, state)
            state = new if turn == PASSES - 1 else {**new, **known(turn + 1)}
        for x in range(8):
            field[x, rows, :] = state[4 + x][0]
        return _

    lax.fori_loop(0, LEV // CHUNK, begin, 0)
    for copy in far:
        copy.wait()
    lax.fori_loop(0, 4 - NEAR, faces, 0)
    lax.fori_loop(11 + NEAR, 15, faces, 0)
    for copy in borders:
        copy.wait()
    lax.fori_loop(0, LEV // CHUNK_END, finish, 0)

    whole = jnp.concatenate([field[x] for x in range(8)], axis=1)
    result = mul_terms(corr_v, whole)
    for x in range(8):
        out_v[pl.ds(x, LEV, stride=8), :] = ext[4 + x, 2] * result[:, x * LANES : (x + 1) * LANES]

    wait_bytes(sums_r.at[:, early_rows], all_send.at[0], group - 1)
    wait_bytes(sums_r.at[:, late_rows], all_send.at[1], group - 1)
    for ref, k in parts:
        wait_bytes(ref, all_send.at[k], nz - 1)
    wait_bytes(tile_r.at[:, first_rows], all_send.at[4], group - 1)


def local(
    nz,
    ng,
    obs_values,
    obs_weight,
    obs_box,
    obs_owner,
    block_count,
    diff_x,
    diff_y,
    spread_std,
    land_sea,
    vert_corr,
):
    group = 2 * ng
    per = LEV // ng
    rows3 = -(-per // 8) * 8
    hbm = pl.BlockSpec(memory_space=pltpu.HBM)
    dma = pltpu.SemaphoreType.DMA
    flat = (LEV * 8, LANES)
    out = pl.pallas_call(
        functools.partial(kernel, nz, ng),
        out_shape=jax.ShapeDtypeStruct(flat, F32),
        in_specs=[pl.BlockSpec(memory_space=pltpu.SMEM)] + [hbm] * 9,
        out_specs=pl.BlockSpec(memory_space=pltpu.VMEM),
        scratch_shapes=[
            pltpu.VMEM((16, LANES), F32),
            pltpu.VMEM((16, LANES), jnp.int32),
            pltpu.SMEM((16,), jnp.int32),
            pltpu.VMEM((8, LANES), jnp.int32),
            pltpu.VMEM((LEV, LEV), F32),
            pltpu.VMEM((16, LEV, LANES), BF16),
            pltpu.VMEM((3,) + flat, F32),
            pltpu.VMEM((16, 3, LEV, LANES), F32),
            pltpu.VMEM((16, 3, LEV, LANES), F32),
            pltpu.VMEM((2, 2, LEV, LANES), F32),
            pltpu.VMEM((2, 2, LEV, LANES), F32),
            pltpu.VMEM((2, LEV, LANES), F32),
            pltpu.VMEM((2, LEV, LANES), F32),
            pltpu.VMEM((group, per * 8 + 1, LANES), F32),
            pltpu.VMEM((group, per * 8 + 1, LANES), F32),
            pltpu.VMEM((2,) + flat, F32),
            pltpu.VMEM((nz, per, ng, LANES), F32),
            pltpu.VMEM((nz, per, ng, LANES), F32),
            pltpu.VMEM((group * rows3, LANES), F32),
            pltpu.VMEM((group, rows3, LANES), F32),
            pltpu.VMEM((2, LEV, LANES), F32),
            pltpu.VMEM((2, LEV, LANES), F32),
            pltpu.VMEM((8, LEV, LANES), F32),
            pltpu.VMEM((16, 2, LEV, LANES), F32),
            pltpu.VMEM((PASSES, 8, 2, LEV, LANES), F32),
            dma((9,)),
            dma((2, 2)),
            dma((2, 2)),
            dma((3,)),
            dma((3,)),
            dma((2,)),
            dma((2,)),
            dma((2,)),
            dma((2,)),
            dma((5,)),
            dma((5,)),
            dma((2,)),
            dma((2,)),
        ],
        compiler_params=pltpu.CompilerParams(
            collective_id=0, has_side_effects=True, vmem_limit_bytes=40 * 1024 * 1024
        ),
        name="analysis",
    )(
        block_count,
        *(
            pltpu.with_memory_space_constraint(value, pltpu.HBM)
            for value in (
                obs_values,
                obs_weight,
                obs_box,
                obs_owner,
                diff_x.reshape(flat),
                diff_y.reshape(flat),
                spread_std.reshape(flat),
                land_sea,
                vert_corr,
            )
        ),
    )
    return out.reshape(LEV, 8, LANES)


def solution(mesh):
    in_specs = (
        P(("gx", "gy"), None, None),
        P(("gx", "gy"), None),
        P(("gx", "gy"), None),
        P(("gx", "gy")),
        P(("gx", "gy")),
        P(None, "gx", "gy"),
        P(None, "gx", "gy"),
        P(None, "gx", "gy"),
        P("gx", "gy"),
        P(),
    )
    return jax.shard_map(
        functools.partial(local, mesh.shape["gx"] // 2, mesh.shape["gy"]),
        mesh=mesh,
        in_specs=in_specs,
        out_specs=P(None, "gx", "gy"),
        check_vma=False,
    )
```
